128 devices in a mesh: req: 4 (over z), tile: 8 (over y, core), span: 4 (over x).
Axes of the slice: x: 4, y: 4, z: 4, core: 2. Of those that a mesh axis runs over, the one named last changes fastest.
Arguments:
- latents: bfloat16 [32, 64, 128, 512], P(('req', 'span'), 'tile'), may hold values from -12 to 12
- frame_counts: int32 [4], replicated, may hold values from 1 to 16, 32 in all
- norm_gain: float32 [512], replicated, may hold values from 0.1 to 1.9
- norm_shift: float32 [512], replicated, may hold values from -3 to 3
- conv_weight: bfloat16 [3, 3, 3, 512, 512], replicated, may hold values from -0.0546875 to 0.0546875
- conv_bias: float32 [512], replicated, may hold values from -2 to 2
Outputs:
- decoded: bfloat16 [32, 64, 128, 512], P(('req', 'span'), 'tile')
The draws below stay inside these ranges and needn't reach their ends.
Inputs may be any that keep to these rules, and one draw needn't show every extreme that they name: `frame_counts`: the 4 counts sum to 32, and the largest is exactly 16.
All inputs are finite; a program needn't handle non-finite values.
Results may differ from the reference program's by a relative error of at most 0.0031.
Values may be sent and summed in bfloat16 or wider, within the bound.
No kernel may reach another device: no remote copies, remote signals or barrier semaphores. Data moves between devices by JAX's collectives and lax.ppermute only.
A program may use at most 192 MiB of HBM per device.

```python
import math
import jax
import jax.numpy as jnp
import numpy as np
from jax import lax

C = 512
GROUPS = 32
REQS = 4
W = 128
FRAMES = 32
ROWS = 64


def draw_latents(key, part):
    noise_key, scale_key = jax.random.split(jax.random.fold_in(key, 17), 2)
    noise = jax.random.normal(noise_key, (FRAMES, ROWS, W, C), jnp.float32)
    frame_rise = (jnp.arange(FRAMES, dtype=jnp.float32) / max(FRAMES - 1, 1)).reshape(FRAMES, 1, 1, 1)
    row_rise = (jnp.arange(ROWS, dtype=jnp.float32) / max(ROWS - 1, 1)).reshape(1, ROWS, 1, 1)
    jitter = jax.random.uniform(scale_key, (FRAMES, ROWS, 1, 1), jnp.float32, 0.8, 1.25)
    scale = 0.6 * jnp.exp(0.5 * math.log(3.0) * (frame_rise + row_rise)) * jitter
    return jnp.clip(scale * noise, -12.0, 12.0).astype(jnp.bfloat16)


def profile(amount, total, limit, skew):
    portions = [(1 << 20) // math.isqrt(standing ** skew) + 1 for standing in range(2, amount + 1)]
    spare, holding = total - limit - (amount - 1), [1] * (amount - 1)
    while spare > 0:
        candidates = [i for i in range(amount - 1) if holding[i] < limit]
        whole, remaining = sum([portions[i] for i in candidates]), spare
        for i in candidates:
            more = min(limit - holding[i], max(1, remaining * portions[i] // whole), spare)
            holding[i] = holding[i] + more
            spare = spare - more
    return np.array([limit] + holding)


def ragged_sizes(key, amount, total, most, slope):
    if amount == 2:
        one = jax.random.randint(key, (), max(1, total - most), min(most, total - 1) + 1)
        return jnp.stack([one, total - one])
    tallies = jnp.asarray(profile(amount, total, most, slope), jnp.int32)
    pairs = (amount - 1) // 2
    giver, receiver = tallies[1:1 + 2 * pairs:2], tallies[2:2 + 2 * pairs:2]
    room = jnp.minimum(giver - 1, most - receiver)
    moved = jax.random.randint(jax.random.fold_in(key, 1), (pairs,), 0, 1 << 20) % (room + 1)
    tallies = tallies.at[1:1 + 2 * pairs:2].set(giver - moved).at[2:2 + 2 * pairs:2].set(receiver + moved)
    return tallies[jax.random.permutation(jax.random.fold_in(key, 2), amount)]


def scatter_about(key, extent, scale, most, kind=jnp.bfloat16):
    entries = scale * jax.random.normal(key, extent, jnp.float32)
    return jnp.clip(entries, min=-most, max=most).astype(kind)


def setup_inputs(seed: int = 0) -> dict:
    key_of = jax.random.split(jax.random.key(seed), 7)
    latents = draw_latents(jax.random.fold_in(key_of[6], 71), 0)
    frame_counts = ragged_sizes(key_of[1], REQS, FRAMES, FRAMES // 2, 2).astype(jnp.int32)
    norm_gain = jnp.clip(1.0 + 0.18 * jax.random.normal(key_of[2], (C,), jnp.float32), 0.1, 1.9)
    norm_shift = scatter_about(key_of[3], (C,), 0.5, 3.0, jnp.float32)
    conv_weight = scatter_about(key_of[4], (3, 3, 3, C, C), (27 * C) ** -0.5, 0.0546875)
    conv_bias = scatter_about(key_of[5], (C,), 0.3, 2.0, jnp.float32)
    return dict(latents=latents, frame_counts=frame_counts, norm_gain=norm_gain, norm_shift=norm_shift, conv_weight=conv_weight, conv_bias=conv_bias)


EPSILON = 1e-06

def membership(positions, request_start, request_end):
    return (positions[:, None] >= request_start[None, :]) & (positions[:, None] < request_end[None, :])

def normalize(source, positions, request_start, request_end, group_mean, group_scale, norm_gain, norm_shift):
    inside = membership(positions, request_start, request_end).astype(jnp.float32)
    per_group = source.shape[-1] // group_mean.shape[1]
    frame_mean = jnp.repeat(jnp.dot(inside, group_mean, precision=lax.Precision.HIGHEST), per_group, axis=1)
    frame_scale = jnp.repeat(jnp.dot(inside, group_scale, precision=lax.Precision.HIGHEST), per_group, axis=1)
    centred = (source.astype(jnp.float32) - frame_mean[:, None, None, :]) * frame_scale[:, None, None, :]
    return jax.nn.silu(centred * norm_gain + norm_shift).astype(jnp.bfloat16)

def reference(latents, frame_counts, norm_gain, norm_shift, conv_weight, conv_bias):
    frame_count, row_count, col_count, channels = latents.shape
    per_group = channels // GROUPS
    request_end = jnp.cumsum(frame_counts).astype(jnp.int32)
    request_start = (request_end - frame_counts).astype(jnp.int32)
    positions = jnp.arange(frame_count, dtype=jnp.int32)
    inside = membership(positions, request_start, request_end)
    values = latents.astype(jnp.float32)
    group_sums = lax.optimization_barrier(jnp.sum(values, axis=(1, 2))).reshape(frame_count, GROUPS, per_group).sum(-1)
    group_squares = lax.optimization_barrier(jnp.sum(values * values, axis=(1, 2))).reshape(frame_count, GROUPS, per_group).sum(-1)
    weights_in = inside.astype(jnp.float32)
    total_sums = jnp.dot(weights_in.T, group_sums, precision=lax.Precision.HIGHEST)
    total_squares = jnp.dot(weights_in.T, group_squares, precision=lax.Precision.HIGHEST)
    cell_count = (frame_counts * (row_count * col_count * per_group)).astype(jnp.float32)[:, None]
    group_mean = total_sums / cell_count
    group_scale = lax.rsqrt(total_squares / cell_count - group_mean * group_mean + EPSILON)
    hidden = normalize(latents, positions, request_start, request_end, group_mean, group_scale, norm_gain, norm_shift)
    padded = jnp.pad(hidden, ((0, 0), (1, 1), (1, 1), (0, 0)), mode='edge')
    frame_start = lax.optimization_barrier(jnp.sum(jnp.where(inside, request_start[None, :], 0), axis=1)).astype(jnp.int32)
    tap_index = jnp.stack([jnp.maximum(positions - 2 + time_tap, frame_start) for time_tap in range(3)], axis=1)

    def one_frame(frame_taps):
        accumulated = jnp.zeros((row_count * col_count, channels), jnp.float32)
        for time_tap in range(3):
            chosen = jnp.take(padded, frame_taps[time_tap], axis=0)
            for row_tap in range(3):
                stacked = jnp.concatenate([chosen[row_tap:row_tap + row_count, col_tap:col_tap + col_count] for col_tap in range(3)], axis=-1)
                kernel = conv_weight[time_tap, row_tap].reshape(3 * channels, channels)
                accumulated = accumulated + jnp.dot(stacked.reshape(row_count * col_count, 3 * channels), kernel, preferred_element_type=jnp.float32)
        return accumulated.reshape(row_count, col_count, channels)
    conv = lax.map(one_frame, tap_index)
    return (values + conv + conv_bias).astype(jnp.bfloat16)
```

```python
import functools

import jax
import jax.numpy as jnp
from jax import lax
from jax.experimental import pallas as pl
from jax.experimental.pallas import tpu as pltpu
from jax.sharding import PartitionSpec as P

GROUPS = 32
EPSILON = 1e-06
LANES = 128
HIGHEST = lax.Precision.HIGHEST

REQ_OF = 0
SOURCE_0 = 4
SOURCE_1 = 6
IS_TOP = 8
IS_BOTTOM = 9
CORE = 10
COUNTS = 11


def group_matrix(channels, per_group, transpose):
    shape = (LANES, channels) if transpose else (channels, LANES)
    lane = lax.broadcasted_iota(jnp.int32, shape, 0 if transpose else 1)
    channel = lax.broadcasted_iota(jnp.int32, shape, 1 if transpose else 0)
    return (channel // per_group == lane).astype(jnp.float32)


def stats_kernel(per_group, scalars, x_ref, out_ref):
    frame = pl.program_id(0)
    rows, cols, channels = x_ref.shape[1:]

    def one_row(i, carry):
        total, squares = carry
        v = x_ref[0, i].astype(jnp.float32).reshape(cols // 8, 8, channels)
        return total + jnp.sum(v, axis=0), squares + jnp.sum(v * v, axis=0)

    zero = jnp.zeros((8, channels), jnp.float32)
    total, squares = lax.fori_loop(0, rows, one_row, (zero, zero))
    members = group_matrix(channels, per_group, False)
    grouped = [
        jnp.sum(
            lax.dot(part, members, precision=HIGHEST, preferred_element_type=jnp.float32),
            axis=0,
            keepdims=True,
        )
        for part in (total, squares)
    ]
    row = lax.broadcasted_iota(jnp.int32, (8, LANES), 0)
    request = scalars[REQ_OF + 2 + frame]
    mine = jnp.where(row == request, grouped[0], 0.0) + jnp.where(
        row == request + 4, grouped[1], 0.0
    )

    @pl.when(frame == 0)
    def _():
        out_ref[...] = mine

    @pl.when(frame != 0)
    def _():
        out_ref[...] += mine


def local_stats(scalars, latents, per_group):
    frames, rows, cols, channels = latents.shape
    return pl.pallas_call(
        functools.partial(stats_kernel, per_group),
        grid_spec=pltpu.PrefetchScalarGridSpec(
            num_scalar_prefetch=1,
            grid=(frames,),
            in_specs=[pl.BlockSpec((1, rows, cols, channels), lambda f, s: (f, 0, 0, 0))],
            out_specs=pl.BlockSpec((8, LANES), lambda f, s: (0, 0)),
        ),
        out_shape=jax.ShapeDtypeStruct((8, LANES), jnp.float32),
        name="local_stats",
    )(scalars, latents)


def affine_of(scalars, total, gain, shift, cells_per_frame, per_group):
    channels = gain.shape[1]
    row = lax.broadcasted_iota(jnp.int32, (4, LANES), 0)
    frames = jnp.zeros((4, LANES), jnp.float32)
    for r in range(4):
        frames = jnp.where(row == r, scalars[COUNTS + r].astype(jnp.float32), frames)
    cells = frames * float(cells_per_frame)
    mean = total[0:4] / cells
    scale = lax.rsqrt(total[4:8] / cells - mean * mean + EPSILON)
    spread = group_matrix(channels, per_group, True)
    both = lax.dot(
        jnp.concatenate([mean, scale], axis=0),
        spread,
        precision=HIGHEST,
        preferred_element_type=jnp.float32,
    )
    factor = both[4:8] * gain
    return jnp.concatenate([factor, shift - both[0:4] * factor], axis=0)


def normalize_rows(raw, stacked, slot, rows, factor, term):
    cols, channels = raw.shape[2:]
    place = lax.broadcasted_iota(jnp.int32, (cols, channels), 0)
    for i in rows:
        u = raw[slot, i].astype(jnp.float32) * factor + term
        h = u * jnp.tanh(u) + u
        left = jnp.where(place == 0, h, pltpu.roll(h, 1, 0))
        right = jnp.where(place == cols - 1, h, pltpu.roll(h, cols - 1, 0))
        stacked[slot, i, :, 0:channels] = left.astype(jnp.bfloat16)
        stacked[slot, i, :, channels : 2 * channels] = h.astype(jnp.bfloat16)
        stacked[slot, i, :, 2 * channels :] = right.astype(jnp.bfloat16)


def conv_kernel(stage, cells_per_frame, per_group, *refs):
    refs = list(refs)
    take = lambda n: [refs.pop(0) for _ in range(n)]
    (scalars,) = take(1)
    lat, top, bottom = take(3)
    rem, edge, inner = take(3) if stage != "a" else (None, None, None)
    (weight,) = take(1)
    if stage == "a":
        total_ref, gain_ref, shift_ref = take(3)
        affine_out, acc_out = take(2)
    elif stage == "b":
        affine_in, bias_ref, acc_in = take(3)
        acc_out, decoded = take(2)
    else:
        affine_in, bias_ref, acc_in, _ = take(4)
        (decoded,) = take(1)
    raw, stacked, kernels, acc, affine, out_tile, io_sem, w_sem = refs
    rows, cols, channels = lat.shape[1:]
    cells = rows * cols

    if stage == "a":
        sources = [2, 3]
        local_only = True
        second = scalars[SOURCE_1 + 1] - 2
        plan = [(0, 2, 0), (1, 2, 1), (1, 1, second)]
    elif stage == "b":
        sources = [scalars[SOURCE_0 + 1], scalars[SOURCE_1]]
        local_only = False
        plan = [(0, 1, 0), (1, 0, 1)]
    else:
        sources = [scalars[SOURCE_0]]
        local_only = False
        plan = [(0, 0, 0)]

    is_top = scalars[IS_TOP] == 1
    is_bottom = scalars[IS_BOTTOM] == 1
    first_core = scalars[CORE] == 0

    def copy(src, dst, sem):
        return pltpu.make_async_copy(src, dst, sem)

    def pick(cond, yes, no):
        @pl.when(cond)
        def _():
            yes()

        @pl.when(jnp.logical_not(cond))
        def _():
            no()

    def load(slot, frame):
        main, upper, lower = (raw.at[slot, pl.ds(1, rows)], raw.at[slot, 0], raw.at[slot, rows + 1])
        sems = (io_sem.at[slot, 0], io_sem.at[slot, 1], io_sem.at[slot, 2])

        def from_local():
            k = frame - 2
            copy(lat.at[k], main, sems[0]).start()
            pick(
                is_top,
                lambda: copy(lat.at[k, 0], upper, sems[1]).start(),
                lambda: copy(top.at[k], upper, sems[1]).start(),
            )
            pick(
                is_bottom,
                lambda: copy(lat.at[k, rows - 1], lower, sems[2]).start(),
                lambda: copy(bottom.at[k], lower, sems[2]).start(),
            )

        def from_remote():
            copy(rem.at[frame], main, sems[0]).start()
            pick(
                is_top,
                lambda: copy(rem.at[frame, 0], upper, sems[1]).start(),
                lambda: pick(
                    first_core,
                    lambda: copy(edge.at[frame], upper, sems[1]).start(),
                    lambda: copy(inner.at[frame], upper, sems[1]).start(),
                ),
            )
            pick(
                is_bottom,
                lambda: copy(rem.at[frame, rows - 1], lower, sems[2]).start(),
                lambda: pick(
                    first_core,
                    lambda: copy(inner.at[frame], lower, sems[2]).start(),
                    lambda: copy(edge.at[frame], lower, sems[2]).start(),
                ),
            )

        if local_only:
            from_local()
        else:
            pick(frame >= 2, from_local, from_remote)

    def loaded(slot):
        main, upper, lower = (raw.at[slot, pl.ds(1, rows)], raw.at[slot, 0], raw.at[slot, rows + 1])
        copy(lat.at[0], main, io_sem.at[slot, 0]).wait()
        copy(top.at[0], upper, io_sem.at[slot, 1]).wait()
        copy(top.at[0], lower, io_sem.at[slot, 2]).wait()

    load(0, sources[0])
    blocks = []
    for _, a, _ in plan:
        for b in range(3):
            if (a, b) not in blocks:
                blocks.append((a, b))
    copies = []
    for k, (a, b) in enumerate(blocks):
        copies.append(copy(weight.at[a, b], kernels.at[k], w_sem.at[k]))
    copies[0].start()
    if len(sources) > 1:
        load(1, sources[1])
    for c in copies[1:]:
        c.start()
    if stage != "a":
        acc_copies = [copy(acc_in.at[o], acc.at[o], io_sem.at[o, 3]) for o in range(acc.shape[0])]
        for c in acc_copies:
            c.start()

    if stage == "a":
        affine[...] = affine_of(
            scalars, total_ref[...], gain_ref[...], shift_ref[...], cells_per_frame, per_group
        )
        affine_out[...] = affine[...]
    else:
        affine[...] = affine_in[...]

    def params(frame):
        request = scalars[REQ_OF + frame]
        factor = affine[pl.ds(request, 1), :] * 0.5
        term = affine[pl.ds(request + 4, 1), :] * 0.5
        return factor, term

    loaded(0)
    normalize_rows(raw, stacked, 0, range(rows + 2), *params(sources[0]))
    waited = set()
    started = set()
    for step, (o, a, slot) in enumerate(plan):
        ahead = step == 0 and len(sources) > 1
        if ahead:
            loaded(1)
            factor, term = params(sources[1])
        if stage != "a" and o not in started:
            acc_copies[o].wait()
            started.add(o)
        for b in range(3):
            k = blocks.index((a, b))
            if k not in waited:
                copies[k].wait()
                waited.add(k)
            for half in range(2):
                unit = 2 * b + half
                span = slice(half * (channels // 2), (half + 1) * (channels // 2))
                part = jnp.dot(
                    stacked[slot, b : b + rows].reshape(cells, 3 * channels),
                    kernels[k, :, span],
                    preferred_element_type=jnp.float32,
                )
                if o in started or b > 0:
                    acc[o, :, span] += part
                else:
                    acc[o, :, span] = part
                if ahead:
                    turn = range(2 * unit, min(2 * unit + 2, rows + 2))
                    normalize_rows(raw, stacked, 1, turn, factor, term)
        started.add(o)

    def finish(o):
        c = copy(lat.at[o], raw.at[0, pl.ds(1, rows)], io_sem.at[0, 0])
        c.start()
        c.wait()
        for i in range(rows):
            value = raw[0, 1 + i].astype(jnp.float32) + acc[o, i * cols : (i + 1) * cols]
            out_tile[i] = (value + bias_ref[...]).astype(jnp.bfloat16)
        c = copy(out_tile, decoded.at[o], io_sem.at[0, 1])
        c.start()
        c.wait()

    if stage == "a":
        outs = [copy(acc.at[o], acc_out.at[o], io_sem.at[o, 3]) for o in range(2)]
        for c in outs:
            c.start()
        for c in outs:
            c.wait()
    elif stage == "b":
        c = copy(acc.at[0], acc_out.at[0], io_sem.at[0, 3])
        c.start()
        finish(1)
        c.wait()
    else:
        finish(0)


def conv_stage(stage, scalars, latents, extras, weight, small, acc=None, decoded=None, per_group=16, cells_per_frame=0):
    frames, rows, cols, channels = latents.shape
    any_spec = pl.BlockSpec(memory_space=pl.ANY)
    vmem = pl.BlockSpec(memory_space=pltpu.VMEM)
    args = [scalars, latents, *extras, weight, *small]
    specs = [pl.BlockSpec(memory_space=pltpu.SMEM)] + [any_spec] * (2 + len(extras)) + [vmem] * len(small)
    aliases = {}
    if acc is not None:
        args.append(acc)
        specs.append(any_spec)
    acc_shape = lambda n: jax.ShapeDtypeStruct((n, rows * cols, channels), jnp.float32)
    out_shape = jax.ShapeDtypeStruct(latents.shape, jnp.bfloat16)
    if stage == "a":
        outs = (jax.ShapeDtypeStruct((8, channels), jnp.float32), acc_shape(2))
        out_specs = (vmem, any_spec)
        slots, blocks, held = 2, 6, 2
    elif stage == "b":
        outs = (acc_shape(1), out_shape)
        out_specs = (any_spec, any_spec)
        slots, blocks, held = 2, 6, 2
    else:
        aliases = {len(args): 0}
        args.append(decoded)
        specs.append(any_spec)
        outs = out_shape
        out_specs = any_spec
        slots, blocks, held = 1, 3, 1
    return pl.pallas_call(
        functools.partial(conv_kernel, stage, cells_per_frame, per_group),
        in_specs=specs,
        out_specs=out_specs,
        out_shape=outs,
        input_output_aliases=aliases,
        scratch_shapes=[
            pltpu.VMEM((slots, rows + 2, cols, channels), jnp.bfloat16),
            pltpu.VMEM((slots, rows + 2, cols, 3 * channels), jnp.bfloat16),
            pltpu.VMEM((blocks, 3 * channels, channels), jnp.bfloat16),
            pltpu.VMEM((held, rows * cols, channels), jnp.float32),
            pltpu.VMEM((8, channels), jnp.float32),
            pltpu.VMEM((rows, cols, channels), jnp.bfloat16),
            pltpu.SemaphoreType.DMA((2, 4)),
            pltpu.SemaphoreType.DMA((blocks,)),
        ],
        compiler_params=pltpu.CompilerParams(vmem_limit_bytes=56 << 20),
        name="conv_" + stage,
    )(*args)


def pair(axis, partner):
    return [(i, partner(i)) for i in range(lax.axis_size(axis))]


def exchange_sum(value, axis, partner):
    return value + lax.ppermute(value, axis, pair(axis, partner))


def shards(latents, frame_counts, norm_gain, norm_shift, conv_weight, conv_bias):
    frames, rows, cols, channels = latents.shape
    per_group = channels // GROUPS
    spread = ("req", "span")
    request_end = jnp.cumsum(frame_counts)
    request_start = request_end - frame_counts
    first = lax.axis_index(spread) * frames
    tile = lax.axis_index("tile")
    positions = first - 2 + jnp.arange(4, dtype=jnp.int32)
    held = jnp.maximum(positions, 0)
    request = jnp.sum((held[:, None] >= request_end[None, :]).astype(jnp.int32), axis=1)
    start = jnp.sum(
        jnp.where(request[2:, None] == jnp.arange(4)[None, :], request_start[None, :], 0), axis=1
    )
    sources = jnp.maximum(
        positions[2:, None] - 2 + jnp.arange(2, dtype=jnp.int32)[None, :], start[:, None]
    ) - first + 2
    scalars = jnp.concatenate(
        [
            request,
            sources.reshape(-1),
            jnp.stack([tile == 0, tile == lax.axis_size("tile") - 1, tile % 2 == 1]).astype(jnp.int32),
            frame_counts,
        ]
    ).astype(jnp.int32)

    onward = [(i, i + 1) for i in range(lax.axis_size("req") * lax.axis_size("span") - 1)]
    count = lax.axis_size("tile")
    down = [(i, i + 1) for i in range(count - 1)]
    up = [(i + 1, i) for i in range(count - 1)]
    top = lax.ppermute(latents[:, -1], "tile", down)
    bottom = lax.ppermute(latents[:, 0], "tile", up)
    rem = lax.ppermute(latents, spread, onward)
    core = tile % 2
    edge = lax.ppermute(jnp.where(core == 0, top, bottom), spread, onward)
    inner = lax.ppermute(
        jnp.where(core == 0, rem[:, -1], rem[:, 0]), "tile", [(i, i ^ 1) for i in range(count)]
    )

    total = local_stats(scalars, latents, per_group)
    for axis in ("tile", "req", "span"):
        step = 1
        while step < lax.axis_size(axis):
            total = exchange_sum(total, axis, lambda i: i ^ step)
            step *= 2

    cells_per_frame = rows * count * cols * per_group
    weight = conv_weight.reshape(3, 3, 3 * channels, channels)
    gain, shift, bias = (v.reshape(1, channels) for v in (norm_gain, norm_shift, conv_bias))
    run = functools.partial(conv_stage, per_group=per_group, cells_per_frame=cells_per_frame)
    near = (top, bottom)
    far = (top, bottom, rem, edge, inner)
    affine, acc = run("a", scalars, latents, near, weight, (total, gain, shift))
    acc, decoded = run("b", scalars, latents, far, weight, (affine, bias), acc)
    return run("c", scalars, latents, far, weight, (affine, bias), acc, decoded)


def solution(mesh):
    placed = (P(("req", "span"), "tile", None, None), P(), P(), P(), P(), P())
    return jax.shard_map(
        shards,
        mesh=mesh,
        in_specs=placed,
        out_specs=P(("req", "span"), "tile", None, None),
        check_vma=False,
    )
```

```python
import functools

import jax
import jax.numpy as jnp
from jax import lax
from jax.experimental import pallas as pl
from jax.experimental.pallas import tpu as pltpu
from jax.sharding import PartitionSpec as P

GROUPS = 32
EPSILON = 1e-06
LANES = 128
HIGHEST = lax.Precision.HIGHEST


def layout(counts, place, frames):
    ends = [counts[0]]
    for r in range(1, 3):
        ends.append(ends[-1] + counts[r])
    first = place[0] * frames

    def request_of(position):
        request = 0
        for end in ends:
            request += (position >= end).astype(jnp.int32)
        return request

    def start_of(position):
        start = 0
        for end in ends:
            start = jnp.where(position >= end, end, start)
        return start

    def request(k):
        return request_of(jnp.maximum(first - 2 + k, 0))

    def source(output, tap):
        position = first + output
        return jnp.maximum(position - 2 + tap, start_of(position)) - first + 2

    return request, source


def group_matrix(channels, per_group, transpose):
    shape = (LANES, channels) if transpose else (channels, LANES)
    lane = lax.broadcasted_iota(jnp.int32, shape, 0 if transpose else 1)
    channel = lax.broadcasted_iota(jnp.int32, shape, 1 if transpose else 0)
    return (channel // per_group == lane).astype(jnp.float32)


def stats_kernel(per_group, frames, counts, place, x_ref, out_ref):
    frame = pl.program_id(0)
    rows, cols, channels = x_ref.shape[1:]

    def one_row(i, carry):
        total, squares = carry
        v = x_ref[0, i].astype(jnp.float32).reshape(cols // 8, 8, channels)
        return total + jnp.sum(v, axis=0), squares + jnp.sum(v * v, axis=0)

    zero = jnp.zeros((8, channels), jnp.float32)
    total, squares = lax.fori_loop(0, rows, one_row, (zero, zero))
    members = group_matrix(channels, per_group, False)
    grouped = [
        jnp.sum(
            lax.dot(part, members, precision=HIGHEST, preferred_element_type=jnp.float32),
            axis=0,
            keepdims=True,
        )
        for part in (total, squares)
    ]
    row = lax.broadcasted_iota(jnp.int32, (8, LANES), 0)
    request = layout(counts, place, frames)[0](2 + frame)
    mine = jnp.where(row == request, grouped[0], 0.0) + jnp.where(
        row == request + 4, grouped[1], 0.0
    )

    @pl.when(frame == 0)
    def _():
        out_ref[...] = mine

    @pl.when(frame != 0)
    def _():
        out_ref[...] += mine


def local_stats(counts, place, latents, per_group):
    frames, rows, cols, channels = latents.shape
    return pl.pallas_call(
        functools.partial(stats_kernel, per_group, frames),
        grid_spec=pltpu.PrefetchScalarGridSpec(
            num_scalar_prefetch=2,
            grid=(frames,),
            in_specs=[pl.BlockSpec((1, rows, cols, channels), lambda f, *_: (f, 0, 0, 0))],
            out_specs=pl.BlockSpec((8, LANES), lambda f, *_: (0, 0)),
        ),
        out_shape=jax.ShapeDtypeStruct((8, LANES), jnp.float32),
        name="local_stats",
    )(counts, place, latents)


def affine_of(counts, total, gain, shift, cells_per_frame, per_group):
    channels = gain.shape[1]
    row = lax.broadcasted_iota(jnp.int32, (4, LANES), 0)
    frames = jnp.zeros((4, LANES), jnp.float32)
    for r in range(4):
        frames = jnp.where(row == r, counts[r].astype(jnp.float32), frames)
    cells = frames * float(cells_per_frame)
    mean = total[0:4] / cells
    scale = lax.rsqrt(total[4:8] / cells - mean * mean + EPSILON)
    spread = group_matrix(channels, per_group, True)
    both = lax.dot(
        jnp.concatenate([mean, scale], axis=0),
        spread,
        precision=HIGHEST,
        preferred_element_type=jnp.float32,
    )
    factor = both[4:8] * gain
    return jnp.concatenate([factor, shift - both[0:4] * factor], axis=0)


def normalize_rows(raw, stacked, slot, rows, factor, term):
    cols, channels = raw.shape[2:]
    place = lax.broadcasted_iota(jnp.int32, (cols, channels), 0)
    for i in rows:
        u = raw[slot, i].astype(jnp.float32) * factor + term
        h = u * jnp.tanh(u) + u
        left = jnp.where(place == 0, h, pltpu.roll(h, 1, 0))
        right = jnp.where(place == cols - 1, h, pltpu.roll(h, cols - 1, 0))
        stacked[slot, i, :, 0:channels] = left.astype(jnp.bfloat16)
        stacked[slot, i, :, channels : 2 * channels] = h.astype(jnp.bfloat16)
        stacked[slot, i, :, 2 * channels :] = right.astype(jnp.bfloat16)


def conv_kernel(stage, cells_per_frame, per_group, *refs):
    refs = list(refs)
    take = lambda n: [refs.pop(0) for _ in range(n)]
    counts, place = take(2)
    lat, top, bottom = take(3)
    if stage != "a":
        near_rows, pair_rows, inner_1 = take(3)
    if stage == "c":
        far_rows, inner_0 = take(2)
    (weight,) = take(1)
    if stage == "a":
        total_ref, gain_ref, shift_ref = take(3)
        affine_out, acc_out = take(2)
    elif stage == "b":
        affine_in, bias_ref, acc_in = take(3)
        acc_out, decoded = take(2)
    else:
        affine_in, bias_ref, acc_in, _ = take(4)
        (decoded,) = take(1)
    raw, stacked, kernels, acc, affine, out_tile, io_sem, w_sem = refs
    rows, cols, channels = lat.shape[1:]
    cells = rows * cols
    request_of, source_of = layout(counts, place, lat.shape[0])
    tile = place[1]

    if stage == "a":
        sources = [2, 3]
        local_only = True
        second = source_of(1, 1) - 2
        plan = [(0, 2, 0), (1, 2, 1), (1, 1, second)]
    elif stage == "b":
        sources = [source_of(0, 1), source_of(1, 0)]
        local_only = False
        plan = [(0, 1, 0), (1, 0, 1)]
    else:
        sources = [source_of(0, 0)]
        local_only = False
        plan = [(0, 0, 0)]

    is_top = tile == 0
    is_bottom = tile == place[2] - 1
    first_core = lax.rem(tile, 2) == 0

    def copy(src, dst, sem):
        return pltpu.make_async_copy(src, dst, sem)

    def pick(cond, yes, no):
        @pl.when(cond)
        def _():
            yes()

        @pl.when(jnp.logical_not(cond))
        def _():
            no()

    def load(slot, frame):
        upper, lower = raw.at[slot, 0], raw.at[slot, rows + 1]
        sems = [io_sem.at[slot, k] for k in range(4)]

        def from_local():
            k = frame - 2
            copy(lat.at[k, pl.ds(0, rows - 1)], raw.at[slot, pl.ds(1, rows - 1)], sems[0]).start()
            copy(lat.at[k, rows - 1], raw.at[slot, rows], sems[3]).start()
            pick(
                is_top,
                lambda: copy(lat.at[k, 0], upper, sems[1]).start(),
                lambda: copy(top.at[k], upper, sems[1]).start(),
            )
            pick(
                is_bottom,
                lambda: copy(lat.at[k, rows - 1], lower, sems[2]).start(),
                lambda: copy(bottom.at[k], lower, sems[2]).start(),
            )

        def from_remote():
            def frame_one():
                def first():
                    copy(near_rows, raw.at[slot, pl.ds(2, rows - 1)], sems[0]).start()
                    copy(pair_rows.at[1], raw.at[slot, 1], sems[3]).start()
                    pick(
                        is_top,
                        lambda: copy(pair_rows.at[1], upper, sems[1]).start(),
                        lambda: copy(pair_rows.at[0], upper, sems[1]).start(),
                    )
                    copy(inner_1.at[0], lower, sems[2]).start()

                def second():
                    copy(near_rows, raw.at[slot, pl.ds(1, rows - 1)], sems[0]).start()
                    copy(pair_rows.at[0], raw.at[slot, rows], sems[3]).start()
                    pick(
                        is_bottom,
                        lambda: copy(pair_rows.at[0], lower, sems[1]).start(),
                        lambda: copy(pair_rows.at[1], lower, sems[1]).start(),
                    )
                    copy(inner_1.at[0], upper, sems[2]).start()

                pick(first_core, first, second)

            def frame_zero():
                body = far_rows.at[pl.ds(1, rows - 1)]
                tail = far_rows.at[pl.ds(0, rows - 1)]

                def first():
                    copy(body, raw.at[slot, pl.ds(1, rows - 1)], sems[0]).start()
                    copy(pair_rows.at[2], raw.at[slot, rows], sems[3]).start()
                    pick(
                        is_top,
                        lambda: copy(far_rows.at[1], upper, sems[1]).start(),
                        lambda: copy(far_rows.at[0], upper, sems[1]).start(),
                    )
                    copy(inner_0.at[0], lower, sems[2]).start()

                def second():
                    copy(tail, raw.at[slot, pl.ds(2, rows - 1)], sems[0]).start()
                    copy(pair_rows.at[2], raw.at[slot, 1], sems[3]).start()
                    pick(
                        is_bottom,
                        lambda: copy(far_rows.at[rows - 2], lower, sems[1]).start(),
                        lambda: copy(far_rows.at[rows - 1], lower, sems[1]).start(),
                    )
                    copy(inner_0.at[0], upper, sems[2]).start()

                pick(first_core, first, second)

            if stage == "b":
                frame_one()
            else:
                pick(frame == 1, frame_one, frame_zero)

        if local_only:
            from_local()
        else:
            pick(frame >= 2, from_local, from_remote)

    def loaded(slot):
        copy(
            lat.at[0, pl.ds(0, rows - 1)], raw.at[slot, pl.ds(1, rows - 1)], io_sem.at[slot, 0]
        ).wait()
        for k, place in ((1, 0), (2, rows + 1), (3, rows)):
            copy(lat.at[0, 0], raw.at[slot, place], io_sem.at[slot, k]).wait()

    load(0, sources[0])
    blocks = []
    for _, a, _ in plan:
        for b in range(3):
            if (a, b) not in blocks:
                blocks.append((a, b))
    copies = []
    for k, (a, b) in enumerate(blocks):
        copies.append(copy(weight.at[a, b], kernels.at[k], w_sem.at[k]))
    copies[0].start()
    if len(sources) > 1:
        load(1, sources[1])
    for c in copies[1:]:
        c.start()
    if stage != "a":
        acc_copies = [copy(acc_in.at[o], acc.at[o], io_sem.at[o, 4]) for o in range(acc.shape[0])]
        for c in acc_copies:
            c.start()

    if stage == "a":
        affine[...] = affine_of(
            counts, total_ref[...], gain_ref[...], shift_ref[...], cells_per_frame, per_group
        )
        affine_out[...] = affine[...]
    else:
        affine[...] = affine_in[...]

    def params(frame):
        request = request_of(frame)
        factor = affine[pl.ds(request, 1), :] * 0.5
        term = affine[pl.ds(request + 4, 1), :] * 0.5
        return factor, term

    loaded(0)
    normalize_rows(raw, stacked, 0, range(rows + 2), *params(sources[0]))
    waited = set()
    started = set()
    for step, (o, a, slot) in enumerate(plan):
        ahead = step == 0 and len(sources) > 1
        if ahead:
            loaded(1)
            factor, term = params(sources[1])
        if stage != "a" and o not in started:
            acc_copies[o].wait()
            started.add(o)
        for b in range(3):
            k = blocks.index((a, b))
            if k not in waited:
                copies[k].wait()
                waited.add(k)
            for half in range(2):
                unit = 2 * b + half
                span = slice(half * (channels // 2), (half + 1) * (channels // 2))
                part = jnp.dot(
                    stacked[slot, b : b + rows].reshape(cells, 3 * channels),
                    kernels[k, :, span],
                    preferred_element_type=jnp.float32,
                )
                if o in started or b > 0:
                    acc[o, :, span] += part
                else:
                    acc[o, :, span] = part
                if ahead:
                    turn = range(2 * unit, min(2 * unit + 2, rows + 2))
                    normalize_rows(raw, stacked, 1, turn, factor, term)
        started.add(o)

    def finish(o):
        c = copy(lat.at[o], raw.at[0, pl.ds(1, rows)], io_sem.at[0, 0])
        c.start()
        c.wait()
        for i in range(rows):
            value = raw[0, 1 + i].astype(jnp.float32) + acc[o, i * cols : (i + 1) * cols]
            out_tile[i] = (value + bias_ref[...]).astype(jnp.bfloat16)
        c = copy(out_tile, decoded.at[o], io_sem.at[0, 1])
        c.start()
        c.wait()

    if stage == "a":
        outs = [copy(acc.at[o], acc_out.at[o], io_sem.at[o, 4]) for o in range(2)]
        for c in outs:
            c.start()
        for c in outs:
            c.wait()
    elif stage == "b":
        c = copy(acc.at[0], acc_out.at[0], io_sem.at[0, 4])
        c.start()
        finish(1)
        c.wait()
    else:
        finish(0)


def conv_stage(stage, counts, place, latents, extras, weight, small, acc=None, decoded=None, per_group=16, cells_per_frame=0):
    _, rows, cols, channels = latents.shape
    any_spec = pl.BlockSpec(memory_space=pl.ANY)
    vmem = pl.BlockSpec(memory_space=pltpu.VMEM)
    args = [counts, place, latents, *extras, weight, *small]
    specs = [pl.BlockSpec(memory_space=pltpu.SMEM)] * 2 + [any_spec] * (2 + len(extras)) + [vmem] * len(small)
    aliases = {}
    if acc is not None:
        args.append(acc)
        specs.append(any_spec)
    acc_shape = lambda n: jax.ShapeDtypeStruct((n, rows * cols, channels), jnp.float32)
    out_shape = jax.ShapeDtypeStruct(latents.shape, jnp.bfloat16)
    if stage == "a":
        outs = (jax.ShapeDtypeStruct((8, channels), jnp.float32), acc_shape(2))
        out_specs = (vmem, any_spec)
        slots, blocks, held = 2, 6, 2
    elif stage == "b":
        outs = (acc_shape(1), out_shape)
        out_specs = (any_spec, any_spec)
        slots, blocks, held = 2, 6, 2
    else:
        aliases = {len(args): 0}
        args.append(decoded)
        specs.append(any_spec)
        outs = out_shape
        out_specs = any_spec
        slots, blocks, held = 1, 3, 1
    return pl.pallas_call(
        functools.partial(conv_kernel, stage, cells_per_frame, per_group),
        in_specs=specs,
        out_specs=out_specs,
        out_shape=outs,
        input_output_aliases=aliases,
        scratch_shapes=[
            pltpu.VMEM((slots, rows + 2, cols, channels), jnp.bfloat16),
            pltpu.VMEM((slots, rows + 2, cols, 3 * channels), jnp.bfloat16),
            pltpu.VMEM((blocks, 3 * channels, channels), jnp.bfloat16),
            pltpu.VMEM((held, rows * cols, channels), jnp.float32),
            pltpu.VMEM((8, channels), jnp.float32),
            pltpu.VMEM((rows, cols, channels), jnp.bfloat16),
            pltpu.SemaphoreType.DMA((2, 5)),
            pltpu.SemaphoreType.DMA((blocks,)),
        ],
        compiler_params=pltpu.CompilerParams(vmem_limit_bytes=56 << 20),
    )(*args)


def shards(latents, frame_counts, norm_gain, norm_shift, conv_weight, conv_bias):
    _, rows, cols, channels = latents.shape
    per_group = channels // GROUPS
    spread = ("req", "span")
    tile = lax.axis_index("tile")
    place = jnp.stack([lax.axis_index(spread), tile, lax.axis_size("tile")]).astype(jnp.int32)

    onward = [(i, i + 1) for i in range(lax.axis_size("req") * lax.axis_size("span") - 1)]
    count = lax.axis_size("tile")
    down = [(i, i + 1) for i in range(count - 1)]
    up = [(i + 1, i) for i in range(count - 1)]
    swap = [(i, i ^ 1) for i in range(count)]
    core = tile % 2
    first_core = core == 0

    def after(value, *others):
        return lax.optimization_barrier((value, *others))[0]

    def fold(value, axis, partner):
        return value + lax.ppermute(value, axis, partner)

    ring = lambda step: [(i, i ^ 1 if step == 0 else 3 - i) for i in range(4)]
    rung = lambda step: [
        (i, 2 * (i // 2 ^ 1 if step == 0 else 3 - i // 2) + i % 2) for i in range(count)
    ]

    near_send = lax.dynamic_slice_in_dim(latents[1], 1 - core, rows - 1, axis=0)
    near_rows = lax.ppermute(near_send, spread, onward)
    total = local_stats(frame_counts, place, latents, per_group)
    total = fold(total, "tile", swap)
    total = fold(total, "tile", rung(0))
    total = fold(total, "tile", rung(1))
    top = lax.ppermute(after(latents[:, -1], total), "tile", down)
    total = fold(total, "req", ring(0))
    bottom = lax.ppermute(after(latents[:, 0], total), "tile", up)
    total = fold(total, "req", ring(1))
    near_rows, total = lax.optimization_barrier((near_rows, total))
    inner_send = jnp.where(first_core, near_rows[rows - 2], near_rows[0])[None]
    inner_1 = lax.ppermute(inner_send, "tile", swap)
    total = fold(total, "span", ring(0))
    pair_send = jnp.where(
        first_core,
        jnp.stack([top[1], latents[1, 0], latents[0, rows - 1]]),
        jnp.stack([latents[1, rows - 1], bottom[1], latents[0, 0]]),
    )
    far_send = jnp.where(
        first_core,
        jnp.concatenate([top[:1], latents[0, : rows - 1]]),
        jnp.concatenate([latents[0, 1:], bottom[:1]]),
    )
    pair_send, far_send, total = lax.optimization_barrier((pair_send, far_send, total))
    other = lax.ppermute(total, "span", ring(1))
    pair_rows = lax.ppermute(pair_send, spread, onward)
    far_rows = lax.ppermute(far_send, spread, onward)
    total = total + other

    cells_per_frame = rows * count * cols * per_group
    weight = conv_weight.reshape(3, 3, 3 * channels, channels)
    gain, shift, bias = (v.reshape(1, channels) for v in (norm_gain, norm_shift, conv_bias))
    run = functools.partial(conv_stage, per_group=per_group, cells_per_frame=cells_per_frame)
    near = (top, bottom)
    middle = (top, bottom, near_rows, pair_rows, inner_1)
    affine, acc = run("a", frame_counts, place, latents, near, weight, (total, gain, shift))
    pair_rows, acc = lax.optimization_barrier((pair_rows, acc))
    inner_0 = lax.ppermute(pair_rows[2:3], "tile", swap)
    acc, decoded = run("b", frame_counts, place, latents, middle[:3] + (pair_rows, inner_1), weight, (affine, bias), acc)
    far = (top, bottom, near_rows, pair_rows, inner_1, far_rows, inner_0)
    return run("c", frame_counts, place, latents, far, weight, (affine, bias), acc, decoded)


def solution(mesh):
    placed = (P(("req", "span"), "tile", None, None), P(), P(), P(), P(), P())
    return jax.shard_map(
        shards,
        mesh=mesh,
        in_specs=placed,
        out_specs=P(("req", "span"), "tile", None, None),
        check_vma=False,
    )
```

```python
import functools

import jax
import jax.numpy as jnp
from jax import lax
from jax.experimental import pallas as pl
from jax.experimental.pallas import tpu as pltpu
from jax.sharding import PartitionSpec as P

GROUPS = 32
EPSILON = 1e-06
EARLY = 5
LANES = 128
HIGHEST = lax.Precision.HIGHEST


def layout(counts, place, frames):
    ends = [counts[0]]
    for r in range(1, 3):
        ends.append(ends[-1] + counts[r])
    first = place[0] * frames

    def request_of(position):
        request = 0
        for end in ends:
            request += (position >= end).astype(jnp.int32)
        return request

    def start_of(position):
        start = 0
        for end in ends:
            start = jnp.where(position >= end, end, start)
        return start

    def request(k):
        return request_of(jnp.maximum(first - 2 + k, 0))

    def source(output, tap):
        position = first + output
        return jnp.maximum(position - 2 + tap, start_of(position)) - first + 2

    return request, source


def group_matrix(channels, per_group, transpose):
    shape = (LANES, channels) if transpose else (channels, LANES)
    lane = lax.broadcasted_iota(jnp.int32, shape, 0 if transpose else 1)
    channel = lax.broadcasted_iota(jnp.int32, shape, 1 if transpose else 0)
    return (channel // per_group == lane).astype(jnp.float32)


def stats_kernel(per_group, frames, counts, place, x_ref, out_ref):
    frame = pl.program_id(0)
    rows, cols, channels = x_ref.shape[1:]

    def one_row(i, carry):
        total, squares = carry
        v = x_ref[0, i].astype(jnp.float32).reshape(cols // 8, 8, channels)
        return total + jnp.sum(v, axis=0), squares + jnp.sum(v * v, axis=0)

    zero = jnp.zeros((8, channels), jnp.float32)
    total, squares = lax.fori_loop(0, rows, one_row, (zero, zero))
    members = group_matrix(channels, per_group, False)
    grouped = [
        jnp.sum(
            lax.dot(part, members, precision=HIGHEST, preferred_element_type=jnp.float32),
            axis=0,
            keepdims=True,
        )
        for part in (total, squares)
    ]
    row = lax.broadcasted_iota(jnp.int32, (8, LANES), 0)
    request = layout(counts, place, frames)[0](2 + frame)
    mine = jnp.where(row == request, grouped[0], 0.0) + jnp.where(
        row == request + 4, grouped[1], 0.0
    )

    @pl.when(frame == 0)
    def _():
        out_ref[...] = mine

    @pl.when(frame != 0)
    def _():
        out_ref[...] += mine


def local_stats(counts, place, latents, per_group):
    frames, rows, cols, channels = latents.shape
    return pl.pallas_call(
        functools.partial(stats_kernel, per_group, frames),
        grid_spec=pltpu.PrefetchScalarGridSpec(
            num_scalar_prefetch=2,
            grid=(frames,),
            in_specs=[pl.BlockSpec((1, rows, cols, channels), lambda f, *_: (f, 0, 0, 0))],
            out_specs=pl.BlockSpec((8, LANES), lambda f, *_: (0, 0)),
        ),
        out_shape=jax.ShapeDtypeStruct((8, LANES), jnp.float32),
        name="local_stats",
    )(counts, place, latents)


def affine_of(counts, total, gain, shift, cells_per_frame, per_group):
    channels = gain.shape[1]
    row = lax.broadcasted_iota(jnp.int32, (4, LANES), 0)
    frames = jnp.zeros((4, LANES), jnp.float32)
    for r in range(4):
        frames = jnp.where(row == r, counts[r].astype(jnp.float32), frames)
    cells = frames * float(cells_per_frame)
    mean = total[0:4] / cells
    scale = lax.rsqrt(total[4:8] / cells - mean * mean + EPSILON)
    spread = group_matrix(channels, per_group, True)
    both = lax.dot(
        jnp.concatenate([mean, scale], axis=0),
        spread,
        precision=HIGHEST,
        preferred_element_type=jnp.float32,
    )
    factor = both[4:8] * gain
    return jnp.concatenate([factor, shift - both[0:4] * factor], axis=0)


def normalize_rows(raw, stacked, slot, rows, factor, term):
    cols, channels = raw.shape[2:]
    place = lax.broadcasted_iota(jnp.int32, (cols, LANES), 0)
    for i in rows:
        for at in range(0, channels, LANES):
            lanes = slice(at, at + LANES)
            u = raw[slot, i, :, lanes].astype(jnp.float32) * factor[:, lanes] + term[:, lanes]
            h = u * jnp.tanh(u) + u
            left = jnp.where(place == 0, h, pltpu.roll(h, 1, 0))
            right = jnp.where(place == cols - 1, h, pltpu.roll(h, cols - 1, 0))
            for tap, value in enumerate((left, h, right)):
                begin = tap * channels + at
                stacked[slot, i, :, begin : begin + LANES] = value.astype(jnp.bfloat16)


def conv_kernel(stage, cells_per_frame, per_group, *refs):
    refs = list(refs)
    take = lambda n: [refs.pop(0) for _ in range(n)]
    counts, place = take(2)
    lat, top, bottom = take(3)
    if stage != "a":
        near_rows, pair_rows, inner_1 = take(3)
    if stage == "c":
        far_rows, inner_0 = take(2)
    (weight,) = take(1)
    if stage == "a":
        total_ref, gain_ref, shift_ref = take(3)
        affine_out, acc_out = take(2)
    elif stage == "b":
        affine_in, bias_ref, acc_in = take(3)
        acc_out, decoded = take(2)
    else:
        affine_in, bias_ref, acc_in, _ = take(4)
        (decoded,) = take(1)
    raw, stacked, kernels, acc, affine, held, residual, io_sem, w_sem, out_sem = refs
    rows, cols, channels = lat.shape[1:]
    cells = rows * cols
    request_of, source_of = layout(counts, place, lat.shape[0])
    tile = place[1]

    if stage == "a":
        sources = [2, 3]
        local_only = True
        second = source_of(1, 1) - 2
        plan = [(0, 2, 0), (1, 2, 1), (1, 1, second)]
    elif stage == "b":
        sources = [source_of(1, 0), source_of(0, 1)]
        local_only = False
        plan = [(1, 0, 0), (0, 1, 1)]
    else:
        sources = [source_of(0, 0)]
        local_only = False
        plan = [(0, 0, 0)]

    is_top = tile == 0
    is_bottom = tile == place[2] - 1
    first_core = lax.rem(tile, 2) == 0

    def copy(src, dst, sem):
        return pltpu.make_async_copy(src, dst, sem)

    def pick(cond, yes, no):
        @pl.when(cond)
        def _():
            yes()

        @pl.when(jnp.logical_not(cond))
        def _():
            no()

    def load(slot, frame):
        upper, lower = raw.at[slot, 0], raw.at[slot, rows + 1]
        sems = [io_sem.at[slot, k] for k in range(4)]

        def from_local():
            k = frame - 2
            copy(lat.at[k, pl.ds(0, rows - 1)], raw.at[slot, pl.ds(1, rows - 1)], sems[0]).start()
            copy(lat.at[k, rows - 1], raw.at[slot, rows], sems[3]).start()
            pick(
                is_top,
                lambda: copy(lat.at[k, 0], upper, sems[1]).start(),
                lambda: copy(top.at[k], upper, sems[1]).start(),
            )
            pick(
                is_bottom,
                lambda: copy(lat.at[k, rows - 1], lower, sems[2]).start(),
                lambda: copy(bottom.at[k], lower, sems[2]).start(),
            )

        def from_remote():
            early = near_rows.shape[0]
            late = rows - early

            def frame_one():
                def first():
                    copy(near_rows, raw.at[slot, pl.ds(late + 1, early)], sems[0]).start()
                    copy(
                        pair_rows.at[pl.ds(2, late - 1)], raw.at[slot, pl.ds(2, late - 1)], sems[0]
                    ).start()
                    copy(pair_rows.at[1], raw.at[slot, 1], sems[3]).start()
                    pick(
                        is_top,
                        lambda: copy(pair_rows.at[1], upper, sems[1]).start(),
                        lambda: copy(pair_rows.at[0], upper, sems[1]).start(),
                    )
                    copy(inner_1.at[0], lower, sems[2]).start()

                def second():
                    copy(near_rows, raw.at[slot, pl.ds(1, early)], sems[0]).start()
                    copy(
                        pair_rows.at[pl.ds(0, late - 1)],
                        raw.at[slot, pl.ds(early + 1, late - 1)],
                        sems[0],
                    ).start()
                    copy(pair_rows.at[late - 1], raw.at[slot, rows], sems[3]).start()
                    pick(
                        is_bottom,
                        lambda: copy(pair_rows.at[late - 1], lower, sems[1]).start(),
                        lambda: copy(pair_rows.at[late], lower, sems[1]).start(),
                    )
                    copy(inner_1.at[0], upper, sems[2]).start()

                pick(first_core, first, second)

            def frame_zero():
                def first():
                    copy(far_rows, raw.at[slot, pl.ds(1, rows - 1)], sems[0]).start()
                    copy(pair_rows.at[late + 2], raw.at[slot, rows], sems[3]).start()
                    pick(
                        is_top,
                        lambda: copy(far_rows.at[0], upper, sems[1]).start(),
                        lambda: copy(pair_rows.at[late + 1], upper, sems[1]).start(),
                    )
                    copy(inner_0.at[0], lower, sems[2]).start()

                def second():
                    copy(far_rows, raw.at[slot, pl.ds(2, rows - 1)], sems[0]).start()
                    copy(pair_rows.at[late + 2], raw.at[slot, 1], sems[3]).start()
                    pick(
                        is_bottom,
                        lambda: copy(far_rows.at[rows - 2], lower, sems[1]).start(),
                        lambda: copy(pair_rows.at[late + 1], lower, sems[1]).start(),
                    )
                    copy(inner_0.at[0], upper, sems[2]).start()

                pick(first_core, first, second)

            if stage == "b":
                frame_one()
            else:
                pick(frame == 1, frame_one, frame_zero)

        if local_only:
            from_local()
        else:
            pick(frame >= 2, from_local, from_remote)

    def loaded(slot):
        copy(
            lat.at[0, pl.ds(0, rows - 1)], raw.at[slot, pl.ds(1, rows - 1)], io_sem.at[slot, 0]
        ).wait()
        for k, place in ((1, 0), (2, rows + 1), (3, rows)):
            copy(lat.at[0, 0], raw.at[slot, place], io_sem.at[slot, k]).wait()

    half_width = channels // 2
    pieces, order = [], []
    for o, a, slot in plan:
        for b in range(3):
            order += [(o, a, slot, half, b) for half in range(2)]
            if (a, b) not in pieces:
                pieces.append((a, b))
    loads = [
        copy(weight.at[a, b], kernels.at[k], w_sem.at[k])
        for k, (a, b) in enumerate(pieces)
    ]
    sent = 0

    def send_until(n):
        nonlocal sent
        while sent < min(n, len(loads)):
            loads[sent].start()
            sent += 1

    load(0, sources[0])
    send_until(1)
    if stage == "a":
        affine[...] = affine_of(
            counts, total_ref[...], gain_ref[...], shift_ref[...], cells_per_frame, per_group
        )
        affine_out[...] = affine[...]
    else:
        affine[...] = affine_in[...]

    def params(frame):
        request = request_of(frame)
        factor = affine[pl.ds(request, 1), :] * 0.5
        term = affine[pl.ds(request + 4, 1), :] * 0.5
        return factor, term

    loaded(0)
    if len(sources) > 1:
        load(1, sources[1])
    send_until(2)
    normalize_rows(raw, stacked, 0, range(rows + 2), *params(sources[0]))

    def held_copy(o):
        return copy(acc_in.at[o], held.at[o], io_sem.at[o, 4])

    def finish(o):
        for i in range(rows):
            for half in range(2):
                span = slice(half * half_width, (half + 1) * half_width)
                value = residual[i, :, span].astype(jnp.float32) + (
                    acc[o, half, i * cols : (i + 1) * cols] + bias_ref[:, span]
                )
                residual[i, :, span] = value.astype(jnp.bfloat16)
            sends.append(copy(residual.at[i], decoded.at[o, i], out_sem.at[i]))
            sends[-1].start()

    sends = []
    waited = set()
    seen = set()
    for step, (o, a, slot, half, b) in enumerate(order):
        ahead = step < 6 and len(sources) > 1
        if step == 0 and ahead:
            loaded(1)
            factor, term = params(sources[1])
        k = pieces.index((a, b))
        if k not in waited:
            loads[k].wait()
            waited.add(k)
            send_until(k + 3)
        if step == 1 and stage != "a":
            for n in {o for o, *_ in plan}:
                held_copy(n).start()
            copy(lat.at[1 if stage == "b" else 0], residual, out_sem.at[rows]).start()
        if step == 3 and stage != "a":
            copy(lat.at[0], residual, out_sem.at[rows]).wait()
        part = jnp.dot(
            stacked[slot, b : b + rows].reshape(cells, 3 * channels),
            kernels[k, :, half * half_width : (half + 1) * half_width],
            preferred_element_type=jnp.float32,
        )
        if stage != "a" and b == 2:
            if half == 0:
                held_copy(o).wait()
            part = part + held[o, half]
        if (o, half) in seen:
            acc[o, half] += part
        else:
            acc[o, half] = part
            seen.add((o, half))
        if ahead:
            turn = range(2 * step, min(2 * step + 2, rows + 2))
            normalize_rows(raw, stacked, 1, turn, factor, term)
        last = not any(x[0] == o and x[3] == half for x in order[step + 1 :])
        if last and (stage == "c" or (stage == "b" and o == 1)):
            if half == 1:
                finish(o)
        elif last:
            sends.append(copy(acc.at[o, half], acc_out.at[o, half], io_sem.at[half, 5 + o]))
            sends[-1].start()
    for c in sends:
        c.wait()


def conv_stage(stage, counts, place, latents, extras, weight, small, acc=None, decoded=None, per_group=16, cells_per_frame=0):
    _, rows, cols, channels = latents.shape
    any_spec = pl.BlockSpec(memory_space=pl.ANY)
    vmem = pl.BlockSpec(memory_space=pltpu.VMEM)
    args = [counts, place, latents, *extras, weight, *small]
    specs = [pl.BlockSpec(memory_space=pltpu.SMEM)] * 2 + [any_spec] * (2 + len(extras)) + [vmem] * len(small)
    aliases = {}
    if acc is not None:
        args.append(acc)
        specs.append(any_spec)
    acc_shape = lambda n: jax.ShapeDtypeStruct((n, 2, rows * cols, channels // 2), jnp.float32)
    out_shape = jax.ShapeDtypeStruct(latents.shape, jnp.bfloat16)
    if stage == "a":
        outs = (jax.ShapeDtypeStruct((8, channels), jnp.float32), acc_shape(2))
        out_specs = (vmem, any_spec)
        slots, blocks, held = 2, 6, 2
    elif stage == "b":
        outs = (acc_shape(1), out_shape)
        out_specs = (any_spec, any_spec)
        slots, blocks, held = 2, 6, 2
    else:
        aliases = {len(args): 0}
        args.append(decoded)
        specs.append(any_spec)
        outs = out_shape
        out_specs = any_spec
        slots, blocks, held = 1, 3, 1
    return pl.pallas_call(
        functools.partial(conv_kernel, stage, cells_per_frame, per_group),
        in_specs=specs,
        out_specs=out_specs,
        out_shape=outs,
        input_output_aliases=aliases,
        scratch_shapes=[
            pltpu.VMEM((slots, rows + 2, cols, channels), jnp.bfloat16),
            pltpu.VMEM((slots, rows + 2, cols, 3 * channels), jnp.bfloat16),
            pltpu.VMEM((blocks, 3 * channels, channels), jnp.bfloat16),
            pltpu.VMEM((held, 2, rows * cols, channels // 2), jnp.float32),
            pltpu.VMEM((8, channels), jnp.float32),
            pltpu.VMEM((held, 2, rows * cols, channels // 2), jnp.float32),
            pltpu.VMEM((rows, cols, channels), jnp.bfloat16),
            pltpu.SemaphoreType.DMA((2, 7)),
            pltpu.SemaphoreType.DMA((blocks,)),
            pltpu.SemaphoreType.DMA((rows + 1,)),
        ],
        compiler_params=pltpu.CompilerParams(vmem_limit_bytes=58 << 20),
    )(*args)


def shards(latents, frame_counts, norm_gain, norm_shift, conv_weight, conv_bias):
    _, rows, cols, channels = latents.shape
    per_group = channels // GROUPS
    spread = ("req", "span")
    tile = lax.axis_index("tile")
    place = jnp.stack([lax.axis_index(spread), tile, lax.axis_size("tile")]).astype(jnp.int32)

    onward = [(i, i + 1) for i in range(lax.axis_size("req") * lax.axis_size("span") - 1)]
    count = lax.axis_size("tile")
    down = [(i, i + 1) for i in range(count - 1)]
    up = [(i + 1, i) for i in range(count - 1)]
    swap = [(i, i ^ 1) for i in range(count)]
    core = tile % 2
    first_core = core == 0

    def after(value, *others):
        return lax.optimization_barrier((value, *others))[0]

    def fold(value, axis, partner):
        return value + lax.ppermute(value, axis, partner)

    ring = lambda step: [(i, i ^ 1 if step == 0 else 3 - i) for i in range(4)]
    rung = lambda step: [
        (i, 2 * (i // 2 ^ 1 if step == 0 else 3 - i // 2) + i % 2) for i in range(count)
    ]

    late = rows - EARLY
    near_send = lax.dynamic_slice_in_dim(latents[1], late * (1 - core), EARLY, axis=0)
    near_rows = lax.ppermute(near_send, spread, onward)
    total = local_stats(frame_counts, place, latents, per_group)
    total = fold(total, "tile", swap)
    total = fold(total, "tile", rung(0))
    total = fold(total, "tile", rung(1))
    top = lax.ppermute(after(latents[:, -1], total), "tile", down)
    total = fold(total, "req", ring(0))
    bottom = lax.ppermute(after(latents[:, 0], total), "tile", up)
    total = fold(total, "req", ring(1))
    total = fold(total, "span", ring(0))
    pair_send = jnp.where(
        first_core,
        jnp.concatenate([top[1:], latents[1, :late], top[:1], latents[0, rows - 1 :]]),
        jnp.concatenate([latents[1, EARLY:], bottom[1:], bottom[:1], latents[0, :1]]),
    )
    far_send = lax.dynamic_slice_in_dim(latents[0], core, rows - 1, axis=0)
    near_rows, total = lax.optimization_barrier((near_rows, total))
    inner_send = jnp.where(first_core, near_rows[EARLY - 1], near_rows[0])[None]
    inner_1 = lax.ppermute(inner_send, "tile", swap)
    other = lax.ppermute(total, "span", ring(1))
    pair_rows = lax.ppermute(pair_send, spread, onward)
    far_rows = lax.ppermute(far_send, spread, onward)
    total = total + other

    cells_per_frame = rows * count * cols * per_group
    weight = conv_weight.reshape(3, 3, 3 * channels, channels)
    gain, shift, bias = (v.reshape(1, channels) for v in (norm_gain, norm_shift, conv_bias))
    run = functools.partial(conv_stage, per_group=per_group, cells_per_frame=cells_per_frame)
    near = (top, bottom)
    middle = (top, bottom, near_rows, pair_rows, inner_1)
    affine, acc = run("a", frame_counts, place, latents, near, weight, (total, gain, shift))
    pair_rows, acc = lax.optimization_barrier((pair_rows, acc))
    inner_0 = lax.ppermute(pair_rows[late + 2 :], "tile", swap)
    acc, decoded = run("b", frame_counts, place, latents, middle[:3] + (pair_rows, inner_1), weight, (affine, bias), acc)
    far = (top, bottom, near_rows, pair_rows, inner_1, far_rows, inner_0)
    return run("c", frame_counts, place, latents, far, weight, (affine, bias), acc, decoded)


def solution(mesh):
    placed = (P(("req", "span"), "tile", None, None), P(), P(), P(), P(), P())
    return jax.shard_map(
        shards,
        mesh=mesh,
        in_specs=placed,
        out_specs=P(("req", "span"), "tile", None, None),
        check_vma=False,
    )
```

```python
import functools

import jax
import jax.numpy as jnp
from jax import lax
from jax.experimental import pallas as pl
from jax.experimental.pallas import tpu as pltpu
from jax.sharding import PartitionSpec as P

GROUPS = 32
EPSILON = 1e-06
EARLY = 5
LANES = 128
HIGHEST = lax.Precision.HIGHEST


def layout(counts, place, frames):
    ends = [counts[0]]
    for r in range(1, 3):
        ends.append(ends[-1] + counts[r])
    first = place[0] * frames

    def request_of(position):
        request = 0
        for end in ends:
            request += (position >= end).astype(jnp.int32)
        return request

    def start_of(position):
        start = 0
        for end in ends:
            start = jnp.where(position >= end, end, start)
        return start

    def request(k):
        return request_of(jnp.maximum(first - 2 + k, 0))

    def source(output, tap):
        position = first + output
        return jnp.maximum(position - 2 + tap, start_of(position)) - first + 2

    return request, source


def group_matrix(channels, per_group, transpose):
    shape = (LANES, channels) if transpose else (channels, LANES)
    lane = lax.broadcasted_iota(jnp.int32, shape, 0 if transpose else 1)
    channel = lax.broadcasted_iota(jnp.int32, shape, 1 if transpose else 0)
    return (channel // per_group == lane).astype(jnp.float32)


def stats_kernel(per_group, frames, counts, place, x_ref, out_ref):
    frame = pl.program_id(0)
    rows, cols, channels = x_ref.shape[1:]

    def one_row(i, carry):
        total, squares = carry
        v = x_ref[0, i].astype(jnp.float32).reshape(cols // 8, 8, channels)
        return total + jnp.sum(v, axis=0), squares + jnp.sum(v * v, axis=0)

    zero = jnp.zeros((8, channels), jnp.float32)
    total, squares = lax.fori_loop(0, rows, one_row, (zero, zero))
    members = group_matrix(channels, per_group, False)
    grouped = [
        jnp.sum(
            lax.dot(part, members, precision=HIGHEST, preferred_element_type=jnp.float32),
            axis=0,
            keepdims=True,
        )
        for part in (total, squares)
    ]
    row = lax.broadcasted_iota(jnp.int32, (8, LANES), 0)
    request = layout(counts, place, frames)[0](2 + frame)
    mine = jnp.where(row == request, grouped[0], 0.0) + jnp.where(
        row == request + 4, grouped[1], 0.0
    )

    @pl.when(frame == 0)
    def _():
        out_ref[...] = mine

    @pl.when(frame != 0)
    def _():
        out_ref[...] += mine


def local_stats(counts, place, latents, per_group):
    frames, rows, cols, channels = latents.shape
    return pl.pallas_call(
        functools.partial(stats_kernel, per_group, frames),
        grid_spec=pltpu.PrefetchScalarGridSpec(
            num_scalar_prefetch=2,
            grid=(frames,),
            in_specs=[pl.BlockSpec((1, rows, cols, channels), lambda f, *_: (f, 0, 0, 0))],
            out_specs=pl.BlockSpec((8, LANES), lambda f, *_: (0, 0)),
        ),
        out_shape=jax.ShapeDtypeStruct((8, LANES), jnp.float32),
        name="local_stats",
    )(counts, place, latents)


def affine_of(counts, total, gain, shift, cells_per_frame, per_group):
    channels = gain.shape[1]
    row = lax.broadcasted_iota(jnp.int32, (4, LANES), 0)
    frames = jnp.zeros((4, LANES), jnp.float32)
    for r in range(4):
        frames = jnp.where(row == r, counts[r].astype(jnp.float32), frames)
    cells = frames * float(cells_per_frame)
    mean = total[0:4] / cells
    scale = lax.rsqrt(total[4:8] / cells - mean * mean + EPSILON)
    spread = group_matrix(channels, per_group, True)
    both = lax.dot(
        jnp.concatenate([mean, scale], axis=0),
        spread,
        precision=HIGHEST,
        preferred_element_type=jnp.float32,
    )
    factor = both[4:8] * gain
    return jnp.concatenate([factor, shift - both[0:4] * factor], axis=0)


def normalize_rows(raw, stacked, slot, rows, factor, term):
    cols, channels = raw.shape[2:]
    place = lax.broadcasted_iota(jnp.int32, (cols, LANES), 0)
    for i in rows:
        for at in range(0, channels, LANES):
            lanes = slice(at, at + LANES)
            u = raw[slot, i, :, lanes].astype(jnp.float32) * factor[:, lanes] + term[:, lanes]
            h = u * jnp.tanh(u) + u
            left = jnp.where(place == 0, h, pltpu.roll(h, 1, 0))
            right = jnp.where(place == cols - 1, h, pltpu.roll(h, cols - 1, 0))
            for tap, value in enumerate((left, h, right)):
                begin = tap * channels + at
                stacked[slot, i, :, begin : begin + LANES] = value.astype(jnp.bfloat16)


def conv_kernel(stage, cells_per_frame, per_group, *refs):
    refs = list(refs)
    take = lambda n: [refs.pop(0) for _ in range(n)]
    counts, place = take(2)
    lat, top, bottom = take(3)
    if stage != "a":
        near_rows, pair_rows, inner_1 = take(3)
    if stage == "c":
        far_rows, inner_0 = take(2)
    (weight,) = take(1)
    if stage == "a":
        total_ref, gain_ref, shift_ref = take(3)
        affine_out, acc_out = take(2)
    elif stage == "b":
        affine_in, bias_ref, acc_in = take(3)
        acc_out, decoded = take(2)
    else:
        affine_in, bias_ref, acc_in, _ = take(4)
        (decoded,) = take(1)
    raw, stacked, kernels, acc, affine, held, residual, io_sem, w_sem, out_sem = refs
    rows, cols, channels = lat.shape[1:]
    request_of, source_of = layout(counts, place, lat.shape[0])
    tile = place[1]

    if stage == "a":
        sources = [2, 3]
        local_only = True
        second = source_of(1, 1) - 2
        plan = [(0, 2, 0), (1, 2, 1), (1, 1, second)]
    elif stage == "b":
        sources = [source_of(1, 0), source_of(0, 1)]
        local_only = False
        plan = [(1, 0, 0), (0, 1, 1)]
    else:
        sources = [source_of(0, 0)]
        local_only = False
        plan = [(0, 0, 0)]

    is_top = tile == 0
    is_bottom = tile == place[2] - 1
    first_core = lax.rem(tile, 2) == 0

    def copy(src, dst, sem):
        return pltpu.make_async_copy(src, dst, sem)

    def pick(cond, yes, no):
        @pl.when(cond)
        def _():
            yes()

        @pl.when(jnp.logical_not(cond))
        def _():
            no()

    def load(slot, frame):
        upper, lower = raw.at[slot, 0], raw.at[slot, rows + 1]
        sems = [io_sem.at[slot, k] for k in range(4)]

        def from_local():
            k = frame - 2
            copy(lat.at[k, pl.ds(0, rows - 1)], raw.at[slot, pl.ds(1, rows - 1)], sems[0]).start()
            copy(lat.at[k, rows - 1], raw.at[slot, rows], sems[3]).start()
            pick(
                is_top,
                lambda: copy(lat.at[k, 0], upper, sems[1]).start(),
                lambda: copy(top.at[k], upper, sems[1]).start(),
            )
            pick(
                is_bottom,
                lambda: copy(lat.at[k, rows - 1], lower, sems[2]).start(),
                lambda: copy(bottom.at[k], lower, sems[2]).start(),
            )

        def from_remote():
            early = near_rows.shape[0]
            late = rows - early

            def frame_one():
                def first():
                    copy(near_rows, raw.at[slot, pl.ds(late + 1, early)], sems[0]).start()
                    copy(
                        pair_rows.at[pl.ds(2, late - 1)], raw.at[slot, pl.ds(2, late - 1)], sems[0]
                    ).start()
                    copy(pair_rows.at[1], raw.at[slot, 1], sems[3]).start()
                    pick(
                        is_top,
                        lambda: copy(pair_rows.at[1], upper, sems[1]).start(),
                        lambda: copy(pair_rows.at[0], upper, sems[1]).start(),
                    )
                    copy(inner_1.at[0], lower, sems[2]).start()

                def second():
                    copy(near_rows, raw.at[slot, pl.ds(1, early)], sems[0]).start()
                    copy(
                        pair_rows.at[pl.ds(0, late - 1)],
                        raw.at[slot, pl.ds(early + 1, late - 1)],
                        sems[0],
                    ).start()
                    copy(pair_rows.at[late - 1], raw.at[slot, rows], sems[3]).start()
                    pick(
                        is_bottom,
                        lambda: copy(pair_rows.at[late - 1], lower, sems[1]).start(),
                        lambda: copy(pair_rows.at[late], lower, sems[1]).start(),
                    )
                    copy(inner_1.at[0], upper, sems[2]).start()

                pick(first_core, first, second)

            def frame_zero():
                def first():
                    copy(far_rows, raw.at[slot, pl.ds(1, rows - 1)], sems[0]).start()
                    copy(pair_rows.at[late + 2], raw.at[slot, rows], sems[3]).start()
                    pick(
                        is_top,
                        lambda: copy(far_rows.at[0], upper, sems[1]).start(),
                        lambda: copy(pair_rows.at[late + 1], upper, sems[1]).start(),
                    )
                    copy(inner_0.at[0], lower, sems[2]).start()

                def second():
                    copy(far_rows, raw.at[slot, pl.ds(2, rows - 1)], sems[0]).start()
                    copy(pair_rows.at[late + 2], raw.at[slot, 1], sems[3]).start()
                    pick(
                        is_bottom,
                        lambda: copy(far_rows.at[rows - 2], lower, sems[1]).start(),
                        lambda: copy(pair_rows.at[late + 1], lower, sems[1]).start(),
                    )
                    copy(inner_0.at[0], upper, sems[2]).start()

                pick(first_core, first, second)

            if stage == "b":
                frame_one()
            else:
                pick(frame == 1, frame_one, frame_zero)

        if local_only:
            from_local()
        else:
            pick(frame >= 2, from_local, from_remote)

    def loaded(slot):
        copy(
            lat.at[0, pl.ds(0, rows - 1)], raw.at[slot, pl.ds(1, rows - 1)], io_sem.at[slot, 0]
        ).wait()
        for k, place in ((1, 0), (2, rows + 1), (3, rows)):
            copy(lat.at[0, 0], raw.at[slot, place], io_sem.at[slot, k]).wait()

    upper_rows = rows // 2
    pieces, order, done = [], [], []
    for o, a, slot in plan:
        if any(later[0] == o for later in plan[len(done) + 1 :]):
            order += [(o, a, slot, half, b) for b in range(3) for half in range(2)]
        else:
            order += [(o, a, slot, half, b) for half in range(2) for b in range(3)]
        done.append(o)
        pieces += [(a, b) for b in range(3) if (a, b) not in pieces]
    loads = [
        copy(weight.at[a, b], kernels.at[k], w_sem.at[k])
        for k, (a, b) in enumerate(pieces)
    ]
    sent = 0

    def send_until(n):
        nonlocal sent
        while sent < min(n, len(loads)):
            loads[sent].start()
            sent += 1

    load(0, sources[0])
    send_until(1)
    if stage == "a":
        affine[...] = affine_of(
            counts, total_ref[...], gain_ref[...], shift_ref[...], cells_per_frame, per_group
        )
        affine_out[...] = affine[...]
    else:
        affine[...] = affine_in[...]

    def params(frame):
        request = request_of(frame)
        factor = affine[pl.ds(request, 1), :] * 0.5
        term = affine[pl.ds(request + 4, 1), :] * 0.5
        return factor, term

    loaded(0)
    if len(sources) > 1:
        load(1, sources[1])
    send_until(2)
    begun = params(sources[0])
    normalize_rows(raw, stacked, 0, range(rows - 2), *begun)

    def held_copy(o):
        return copy(acc_in.at[o], held.at[o], io_sem.at[o, 4])

    def finish(o, half):
        if half == 0:
            held_copy(o).wait()
            copy(lat.at[0], residual, out_sem.at[rows]).wait()
        for i in range(upper_rows):
            r = half * upper_rows + i
            cell = slice(i * cols, (i + 1) * cols)
            value = residual[r].astype(jnp.float32) + (
                acc[o, half, cell] + held[o, half, cell] + bias_ref[...]
            )
            residual[r] = value.astype(jnp.bfloat16)
            sends.append(copy(residual.at[r], decoded.at[o, r], out_sem.at[r]))
            sends[-1].start()

    sends, pending = [], []
    waited = set()
    seen = set()
    for step, (o, a, slot, half, b) in enumerate(order):
        ahead = 2 <= step < 6 and len(sources) > 1
        if step == 2 and ahead:
            loaded(1)
            factor, term = params(sources[1])
        k = pieces.index((a, b))
        if k not in waited:
            loads[k].wait()
            waited.add(k)
            send_until(k + 3)
        if step == 0 and stage != "a":
            for n in sorted({o for o, *_ in plan}, reverse=True):
                held_copy(n).start()
            copy(lat.at[1 if stage == "b" else 0], residual, out_sem.at[rows]).start()
        finished = stage == "c" or (stage == "b" and o == 1)
        top_row = half * upper_rows + b
        part = jnp.dot(
            stacked[slot, top_row : top_row + upper_rows].reshape(upper_rows * cols, 3 * channels),
            kernels[k],
            preferred_element_type=jnp.float32,
        )
        if stage != "a" and not finished and b == 2:
            if half == 0:
                held_copy(o).wait()
            part = part + held[o, half]
        if (o, half) in seen:
            acc[o, half] += part
        else:
            acc[o, half] = part
            seen.add((o, half))
        if step < 2:
            normalize_rows(raw, stacked, 0, range(rows - 2 + 2 * step, rows + 2 * step), *begun)
        if ahead:
            turn = range(3 * (step - 2), min(3 * (step - 2) + 3, rows + 2))
            normalize_rows(raw, stacked, 1, turn, factor, term)
        last = not any(x[0] == o and x[3] == half for x in order[step + 1 :])
        if last and finished:
            pending.append((step + 2, o, half))
        elif last:
            sends.append(copy(acc.at[o, half], acc_out.at[o, half], io_sem.at[half, 5 + o]))
            sends[-1].start()
        while pending and (pending[0][0] <= step or step == len(order) - 1):
            finish(*pending.pop(0)[1:])
    for c in sends:
        c.wait()


def conv_stage(stage, counts, place, latents, extras, weight, small, acc=None, decoded=None, per_group=16, cells_per_frame=0):
    _, rows, cols, channels = latents.shape
    any_spec = pl.BlockSpec(memory_space=pl.ANY)
    vmem = pl.BlockSpec(memory_space=pltpu.VMEM)
    args = [counts, place, latents, *extras, weight, *small]
    specs = [pl.BlockSpec(memory_space=pltpu.SMEM)] * 2 + [any_spec] * (2 + len(extras)) + [vmem] * len(small)
    aliases = {}
    if acc is not None:
        args.append(acc)
        specs.append(any_spec)
    acc_shape = lambda n: jax.ShapeDtypeStruct((n, 2, rows * cols // 2, channels), jnp.float32)
    out_shape = jax.ShapeDtypeStruct(latents.shape, jnp.bfloat16)
    if stage == "a":
        outs = (jax.ShapeDtypeStruct((8, channels), jnp.float32), acc_shape(2))
        out_specs = (vmem, any_spec)
        slots, blocks, held = 2, 6, 2
    elif stage == "b":
        outs = (acc_shape(1), out_shape)
        out_specs = (any_spec, any_spec)
        slots, blocks, held = 2, 6, 2
    else:
        aliases = {len(args): 0}
        args.append(decoded)
        specs.append(any_spec)
        outs = out_shape
        out_specs = any_spec
        slots, blocks, held = 1, 3, 1
    return pl.pallas_call(
        functools.partial(conv_kernel, stage, cells_per_frame, per_group),
        in_specs=specs,
        out_specs=out_specs,
        out_shape=outs,
        input_output_aliases=aliases,
        scratch_shapes=[
            pltpu.VMEM((slots, rows + 2, cols, channels), jnp.bfloat16),
            pltpu.VMEM((slots, rows + 2, cols, 3 * channels), jnp.bfloat16),
            pltpu.VMEM((blocks, 3 * channels, channels), jnp.bfloat16),
            pltpu.VMEM((held, 2, rows * cols // 2, channels), jnp.float32),
            pltpu.VMEM((8, channels), jnp.float32),
            pltpu.VMEM((held, 2, rows * cols // 2, channels), jnp.float32),
            pltpu.VMEM((rows, cols, channels), jnp.bfloat16),
            pltpu.SemaphoreType.DMA((2, 7)),
            pltpu.SemaphoreType.DMA((blocks,)),
            pltpu.SemaphoreType.DMA((rows + 1,)),
        ],
        compiler_params=pltpu.CompilerParams(vmem_limit_bytes=58 << 20),
    )(*args)


def shards(latents, frame_counts, norm_gain, norm_shift, conv_weight, conv_bias):
    _, rows, cols, channels = latents.shape
    per_group = channels // GROUPS
    spread = ("req", "span")
    tile = lax.axis_index("tile")
    place = jnp.stack([lax.axis_index(spread), tile, lax.axis_size("tile")]).astype(jnp.int32)

    onward = [(i, i + 1) for i in range(lax.axis_size("req") * lax.axis_size("span") - 1)]
    count = lax.axis_size("tile")
    down = [(i, i + 1) for i in range(count - 1)]
    up = [(i + 1, i) for i in range(count - 1)]
    swap = [(i, i ^ 1) for i in range(count)]
    core = tile % 2
    first_core = core == 0

    def after(value, *others):
        return lax.optimization_barrier((value, *others))[0]

    def fold(value, axis, partner):
        return value + lax.ppermute(value, axis, partner)

    ring = lambda step: [(i, i ^ 1 if step == 0 else 3 - i) for i in range(4)]
    rung = lambda step: [
        (i, 2 * (i // 2 ^ 1 if step == 0 else 3 - i // 2) + i % 2) for i in range(count)
    ]

    late = rows - EARLY
    near_send = lax.dynamic_slice_in_dim(latents[1], late * (1 - core), EARLY, axis=0)
    near_rows = lax.ppermute(near_send, spread, onward)
    total = local_stats(frame_counts, place, latents, per_group)
    total = fold(total, "tile", swap)
    total = fold(total, "tile", rung(0))
    total = fold(total, "tile", rung(1))
    top = lax.ppermute(after(latents[:, -1], total), "tile", down)
    total = fold(total, "req", ring(0))
    bottom = lax.ppermute(after(latents[:, 0], total), "tile", up)
    total = fold(total, "req", ring(1))
    other = lax.ppermute(total, "span", ring(0))
    pair_send = jnp.where(
        first_core,
        jnp.concatenate([top[1:], latents[1, :late], top[:1], latents[0, rows - 1 :]]),
        jnp.concatenate([latents[1, EARLY:], bottom[1:], bottom[:1], latents[0, :1]]),
    )
    far_send = lax.dynamic_slice_in_dim(latents[0], core, rows - 1, axis=0)
    total = total + other
    near_rows, total = lax.optimization_barrier((near_rows, total))
    inner_send = jnp.where(first_core, near_rows[EARLY - 1], near_rows[0])[None]
    inner_1 = lax.ppermute(inner_send, "tile", swap)
    other = lax.ppermute(total, "span", ring(1))
    pair_rows = lax.ppermute(pair_send, spread, onward)
    far_rows = lax.ppermute(far_send, spread, onward)
    total = total + other

    cells_per_frame = rows * count * cols * per_group
    weight = conv_weight.reshape(3, 3, 3 * channels, channels)
    gain, shift, bias = (v.reshape(1, channels) for v in (norm_gain, norm_shift, conv_bias))
    run = functools.partial(conv_stage, per_group=per_group, cells_per_frame=cells_per_frame)
    near = (top, bottom)
    middle = (top, bottom, near_rows, pair_rows, inner_1)
    affine, acc = run("a", frame_counts, place, latents, near, weight, (total, gain, shift))
    pair_rows, acc = lax.optimization_barrier((pair_rows, acc))
    inner_0 = lax.ppermute(pair_rows[late + 2 :], "tile", swap)
    acc, decoded = run("b", frame_counts, place, latents, middle[:3] + (pair_rows, inner_1), weight, (affine, bias), acc)
    far = (top, bottom, near_rows, pair_rows, inner_1, far_rows, inner_0)
    return run("c", frame_counts, place, latents, far, weight, (affine, bias), acc, decoded)


def solution(mesh):
    placed = (P(("req", "span"), "tile", None, None), P(), P(), P(), P(), P())
    return jax.shard_map(
        shards,
        mesh=mesh,
        in_specs=placed,
        out_specs=P(("req", "span"), "tile", None, None),
        check_vma=False,
    )
```

```python
import functools

import jax
import jax.numpy as jnp
from jax import lax
from jax.experimental import pallas as pl
from jax.experimental.pallas import tpu as pltpu
from jax.sharding import PartitionSpec as P

GROUPS = 32
EPSILON = 1e-06
EARLY = 6
LANES = 128
HIGHEST = lax.Precision.HIGHEST


def layout(counts, place, frames):
    ends = [counts[0]]
    for r in range(1, 3):
        ends.append(ends[-1] + counts[r])
    first = place[0] * frames

    def request_of(position):
        request = 0
        for end in ends:
            request += (position >= end).astype(jnp.int32)
        return request

    def start_of(position):
        start = 0
        for end in ends:
            start = jnp.where(position >= end, end, start)
        return start

    def request(k):
        return request_of(jnp.maximum(first - 2 + k, 0))

    def source(output, tap):
        position = first + output
        return jnp.maximum(position - 2 + tap, start_of(position)) - first + 2

    return request, source


def group_matrix(channels, per_group, transpose):
    shape = (LANES, channels) if transpose else (channels, LANES)
    lane = lax.broadcasted_iota(jnp.int32, shape, 0 if transpose else 1)
    channel = lax.broadcasted_iota(jnp.int32, shape, 1 if transpose else 0)
    return (channel // per_group == lane).astype(jnp.float32)


def stats_kernel(per_group, frames, counts, place, x_ref, out_ref):
    frame = pl.program_id(0)
    rows, cols, channels = x_ref.shape[1:]

    def one_row(i, carry):
        total, squares = carry
        v = x_ref[0, i].astype(jnp.float32).reshape(cols // 8, 8, channels)
        return total + jnp.sum(v, axis=0), squares + jnp.sum(v * v, axis=0)

    zero = jnp.zeros((8, channels), jnp.float32)
    total, squares = lax.fori_loop(0, rows, one_row, (zero, zero))
    members = group_matrix(channels, per_group, False)
    grouped = [
        jnp.sum(
            lax.dot(part, members, precision=HIGHEST, preferred_element_type=jnp.float32),
            axis=0,
            keepdims=True,
        )
        for part in (total, squares)
    ]
    row = lax.broadcasted_iota(jnp.int32, (8, LANES), 0)
    request = layout(counts, place, frames)[0](2 + frame)
    mine = jnp.where(row == request, grouped[0], 0.0) + jnp.where(
        row == request + 4, grouped[1], 0.0
    )

    @pl.when(frame == 0)
    def _():
        out_ref[...] = mine

    @pl.when(frame != 0)
    def _():
        out_ref[...] += mine


def local_stats(counts, place, latents, per_group):
    frames, rows, cols, channels = latents.shape
    return pl.pallas_call(
        functools.partial(stats_kernel, per_group, frames),
        grid_spec=pltpu.PrefetchScalarGridSpec(
            num_scalar_prefetch=2,
            grid=(frames,),
            in_specs=[pl.BlockSpec((1, rows, cols, channels), lambda f, *_: (f, 0, 0, 0))],
            out_specs=pl.BlockSpec((8, LANES), lambda f, *_: (0, 0)),
        ),
        out_shape=jax.ShapeDtypeStruct((8, LANES), jnp.float32),
        name="local_stats",
    )(counts, place, latents)


def affine_of(counts, total, gain, shift, cells_per_frame, per_group):
    channels = gain.shape[1]
    row = lax.broadcasted_iota(jnp.int32, (4, LANES), 0)
    frames = jnp.zeros((4, LANES), jnp.float32)
    for r in range(4):
        frames = jnp.where(row == r, counts[r].astype(jnp.float32), frames)
    cells = frames * float(cells_per_frame)
    mean = total[0:4] / cells
    scale = lax.rsqrt(total[4:8] / cells - mean * mean + EPSILON)
    spread = group_matrix(channels, per_group, True)
    both = lax.dot(
        jnp.concatenate([mean, scale], axis=0),
        spread,
        precision=HIGHEST,
        preferred_element_type=jnp.float32,
    )
    factor = both[4:8] * gain
    return jnp.concatenate([factor, shift - both[0:4] * factor], axis=0)


def normalize_rows(raw, stacked, slot, rows, factor, term):
    cols, channels = raw.shape[2:]
    place = lax.broadcasted_iota(jnp.int32, (cols, LANES), 0)
    for i in rows:
        for at in range(0, channels, LANES):
            lanes = slice(at, at + LANES)
            u = raw[slot, i, :, lanes].astype(jnp.float32) * factor[:, lanes] + term[:, lanes]
            h = u * jnp.tanh(u) + u
            left = jnp.where(place == 0, h, pltpu.roll(h, 1, 0))
            right = jnp.where(place == cols - 1, h, pltpu.roll(h, cols - 1, 0))
            for tap, value in enumerate((left, h, right)):
                begin = tap * channels + at
                stacked[slot, i, :, begin : begin + LANES] = value.astype(jnp.bfloat16)


def conv_kernel(stage, cells_per_frame, per_group, *refs):
    refs = list(refs)
    take = lambda n: [refs.pop(0) for _ in range(n)]
    counts, place = take(2)
    lat, top, bottom = take(3)
    if stage != "a":
        near_rows, pair_rows, inner_1 = take(3)
    if stage == "c":
        far_rows, inner_0 = take(2)
    (weight,) = take(1)
    if stage == "a":
        total_ref, gain_ref, shift_ref = take(3)
        affine_out, acc_out = take(2)
    elif stage == "b":
        affine_in, bias_ref, acc_in = take(3)
        acc_out, decoded = take(2)
    else:
        affine_in, bias_ref, acc_in, _ = take(4)
        (decoded,) = take(1)
    raw, stacked, kernels, acc, affine, held, residual, io_sem, w_sem, out_sem = refs
    rows, cols, channels = lat.shape[1:]
    request_of, source_of = layout(counts, place, lat.shape[0])
    tile = place[1]

    if stage == "a":
        sources = [2, 3]
        local_only = True
        second = source_of(1, 1) - 2
        plan = [(0, 2, 0), (1, 2, 1), (1, 1, second)]
    elif stage == "b":
        sources = [source_of(1, 0), source_of(0, 1)]
        local_only = False
        plan = [(1, 0, 0), (0, 1, 1)]
    else:
        sources = [source_of(0, 0)]
        local_only = False
        plan = [(0, 0, 0)]

    is_top = tile == 0
    is_bottom = tile == place[2] - 1
    first_core = lax.rem(tile, 2) == 0

    def copy(src, dst, sem):
        return pltpu.make_async_copy(src, dst, sem)

    def pick(cond, yes, no):
        @pl.when(cond)
        def _():
            yes()

        @pl.when(jnp.logical_not(cond))
        def _():
            no()

    def load(slot, frame):
        upper, lower = raw.at[slot, 0], raw.at[slot, rows + 1]
        sems = [io_sem.at[slot, k] for k in range(4)]

        def from_local():
            k = frame - 2
            copy(lat.at[k, pl.ds(0, rows - 1)], raw.at[slot, pl.ds(1, rows - 1)], sems[0]).start()
            copy(lat.at[k, rows - 1], raw.at[slot, rows], sems[3]).start()
            pick(
                is_top,
                lambda: copy(lat.at[k, 0], upper, sems[1]).start(),
                lambda: copy(top.at[k], upper, sems[1]).start(),
            )
            pick(
                is_bottom,
                lambda: copy(lat.at[k, rows - 1], lower, sems[2]).start(),
                lambda: copy(bottom.at[k], lower, sems[2]).start(),
            )

        def from_remote():
            early = near_rows.shape[0]
            late = rows - early

            def frame_one():
                def first():
                    copy(near_rows, raw.at[slot, pl.ds(late + 1, early)], sems[0]).start()
                    copy(
                        pair_rows.at[pl.ds(2, late - 1)], raw.at[slot, pl.ds(2, late - 1)], sems[0]
                    ).start()
                    copy(pair_rows.at[1], raw.at[slot, 1], sems[3]).start()
                    pick(
                        is_top,
                        lambda: copy(pair_rows.at[1], upper, sems[1]).start(),
                        lambda: copy(pair_rows.at[0], upper, sems[1]).start(),
                    )
                    copy(inner_1.at[0], lower, sems[2]).start()

                def second():
                    copy(near_rows, raw.at[slot, pl.ds(1, early)], sems[0]).start()
                    copy(
                        pair_rows.at[pl.ds(0, late - 1)],
                        raw.at[slot, pl.ds(early + 1, late - 1)],
                        sems[0],
                    ).start()
                    copy(pair_rows.at[late - 1], raw.at[slot, rows], sems[3]).start()
                    pick(
                        is_bottom,
                        lambda: copy(pair_rows.at[late - 1], lower, sems[1]).start(),
                        lambda: copy(pair_rows.at[late], lower, sems[1]).start(),
                    )
                    copy(inner_1.at[0], upper, sems[2]).start()

                pick(first_core, first, second)

            def frame_zero():
                def first():
                    copy(far_rows, raw.at[slot, pl.ds(1, rows - 1)], sems[0]).start()
                    copy(pair_rows.at[late + 2], raw.at[slot, rows], sems[3]).start()
                    pick(
                        is_top,
                        lambda: copy(far_rows.at[0], upper, sems[1]).start(),
                        lambda: copy(pair_rows.at[late + 1], upper, sems[1]).start(),
                    )
                    copy(inner_0.at[0], lower, sems[2]).start()

                def second():
                    copy(far_rows, raw.at[slot, pl.ds(2, rows - 1)], sems[0]).start()
                    copy(pair_rows.at[late + 2], raw.at[slot, 1], sems[3]).start()
                    pick(
                        is_bottom,
                        lambda: copy(far_rows.at[rows - 2], lower, sems[1]).start(),
                        lambda: copy(pair_rows.at[late + 1], lower, sems[1]).start(),
                    )
                    copy(inner_0.at[0], upper, sems[2]).start()

                pick(first_core, first, second)

            if stage == "b":
                frame_one()
            else:
                pick(frame == 1, frame_one, frame_zero)

        if local_only:
            from_local()
        else:
            pick(frame >= 2, from_local, from_remote)

    def loaded(slot):
        copy(
            lat.at[0, pl.ds(0, rows - 1)], raw.at[slot, pl.ds(1, rows - 1)], io_sem.at[slot, 0]
        ).wait()
        for k, place in ((1, 0), (2, rows + 1), (3, rows)):
            copy(lat.at[0, 0], raw.at[slot, place], io_sem.at[slot, k]).wait()

    upper_rows = rows // 2
    pieces, order, done = [], [], []
    for o, a, slot in plan:
        if any(later[0] == o for later in plan[len(done) + 1 :]):
            order += [(o, a, slot, half, b) for b in range(3) for half in range(2)]
        else:
            order += [(o, a, slot, half, b) for half in range(2) for b in range(3)]
        done.append(o)
        pieces += [(a, b) for b in range(3) if (a, b) not in pieces]
    loads = [
        copy(weight.at[a, b], kernels.at[k], w_sem.at[k])
        for k, (a, b) in enumerate(pieces)
    ]
    sent = 0

    def send_until(n):
        nonlocal sent
        while sent < min(n, len(loads)):
            loads[sent].start()
            sent += 1

    load(0, sources[0])
    send_until(1)
    if stage == "a":
        affine[...] = affine_of(
            counts, total_ref[...], gain_ref[...], shift_ref[...], cells_per_frame, per_group
        )
        affine_out[...] = affine[...]
    else:
        affine[...] = affine_in[...]

    def params(frame):
        request = request_of(frame)
        factor = affine[pl.ds(request, 1), :] * 0.5
        term = affine[pl.ds(request + 4, 1), :] * 0.5
        return factor, term

    loaded(0)
    if len(sources) > 1:
        load(1, sources[1])
    send_until(2)
    begun = params(sources[0])
    normalize_rows(raw, stacked, 0, range(rows - 2), *begun)

    def held_copy(o):
        return copy(acc_in.at[o], held.at[o], io_sem.at[o, 4])

    def finish(o, half):
        if half == 0:
            held_copy(o).wait()
            copy(lat.at[0], residual, out_sem.at[rows]).wait()
        for i in range(upper_rows):
            r = half * upper_rows + i
            cell = slice(i * cols, (i + 1) * cols)
            value = residual[r].astype(jnp.float32) + (
                acc[o, half, cell] + held[o, half, cell] + bias_ref[...]
            )
            residual[r] = value.astype(jnp.bfloat16)
            sends.append(copy(residual.at[r], decoded.at[o, r], out_sem.at[r]))
            sends[-1].start()

    sends, pending = [], []
    waited = set()
    seen = set()
    for step, (o, a, slot, half, b) in enumerate(order):
        ahead = 2 <= step < 6 and len(sources) > 1
        if step == 2 and ahead:
            loaded(1)
            factor, term = params(sources[1])
        k = pieces.index((a, b))
        if k not in waited:
            loads[k].wait()
            waited.add(k)
            send_until(k + 3)
        if step == 0 and stage != "a":
            for n in sorted({o for o, *_ in plan}, reverse=True):
                held_copy(n).start()
            copy(lat.at[1 if stage == "b" else 0], residual, out_sem.at[rows]).start()
        finished = stage == "c" or (stage == "b" and o == 1)
        top_row = half * upper_rows + b
        part = jnp.dot(
            stacked[slot, top_row : top_row + upper_rows].reshape(upper_rows * cols, 3 * channels),
            kernels[k],
            preferred_element_type=jnp.float32,
        )
        if stage != "a" and not finished and b == 2:
            if half == 0:
                held_copy(o).wait()
            part = part + held[o, half]
        if (o, half) in seen:
            acc[o, half] += part
        else:
            acc[o, half] = part
            seen.add((o, half))
        if step < 2:
            normalize_rows(raw, stacked, 0, range(rows - 2 + 2 * step, rows + 2 * step), *begun)
        if ahead:
            turn = range(3 * (step - 2), min(3 * (step - 2) + 3, rows + 2))
            normalize_rows(raw, stacked, 1, turn, factor, term)
        last = not any(x[0] == o and x[3] == half for x in order[step + 1 :])
        if last and finished:
            pending.append((step + 2, o, half))
        elif last:
            sends.append(copy(acc.at[o, half], acc_out.at[o, half], io_sem.at[half, 5 + o]))
            sends[-1].start()
        while pending and (pending[0][0] <= step or step == len(order) - 1):
            finish(*pending.pop(0)[1:])
    for c in sends:
        c.wait()


def conv_stage(stage, counts, place, latents, extras, weight, small, acc=None, decoded=None, per_group=16, cells_per_frame=0):
    _, rows, cols, channels = latents.shape
    any_spec = pl.BlockSpec(memory_space=pl.ANY)
    vmem = pl.BlockSpec(memory_space=pltpu.VMEM)
    args = [counts, place, latents, *extras, weight, *small]
    specs = [pl.BlockSpec(memory_space=pltpu.SMEM)] * 2 + [any_spec] * (2 + len(extras)) + [vmem] * len(small)
    aliases = {}
    if acc is not None:
        args.append(acc)
        specs.append(any_spec)
    acc_shape = lambda n: jax.ShapeDtypeStruct((n, 2, rows * cols // 2, channels), jnp.float32)
    out_shape = jax.ShapeDtypeStruct(latents.shape, jnp.bfloat16)
    if stage == "a":
        outs = (jax.ShapeDtypeStruct((8, channels), jnp.float32), acc_shape(2))
        out_specs = (vmem, any_spec)
        slots, blocks, held = 2, 6, 2
    elif stage == "b":
        outs = (acc_shape(1), out_shape)
        out_specs = (any_spec, any_spec)
        slots, blocks, held = 2, 6, 2
    else:
        aliases = {len(args): 0}
        args.append(decoded)
        specs.append(any_spec)
        outs = out_shape
        out_specs = any_spec
        slots, blocks, held = 1, 3, 1
    return pl.pallas_call(
        functools.partial(conv_kernel, stage, cells_per_frame, per_group),
        in_specs=specs,
        out_specs=out_specs,
        out_shape=outs,
        input_output_aliases=aliases,
        scratch_shapes=[
            pltpu.VMEM((slots, rows + 2, cols, channels), jnp.bfloat16),
            pltpu.VMEM((slots, rows + 2, cols, 3 * channels), jnp.bfloat16),
            pltpu.VMEM((blocks, 3 * channels, channels), jnp.bfloat16),
            pltpu.VMEM((held, 2, rows * cols // 2, channels), jnp.float32),
            pltpu.VMEM((8, channels), jnp.float32),
            pltpu.VMEM((held, 2, rows * cols // 2, channels), jnp.float32),
            pltpu.VMEM((rows, cols, channels), jnp.bfloat16),
            pltpu.SemaphoreType.DMA((2, 7)),
            pltpu.SemaphoreType.DMA((blocks,)),
            pltpu.SemaphoreType.DMA((rows + 1,)),
        ],
        compiler_params=pltpu.CompilerParams(vmem_limit_bytes=58 << 20),
    )(*args)


def shards(latents, frame_counts, norm_gain, norm_shift, conv_weight, conv_bias):
    _, rows, cols, channels = latents.shape
    per_group = channels // GROUPS
    spread = ("req", "span")
    tile = lax.axis_index("tile")
    place = jnp.stack([lax.axis_index(spread), tile, lax.axis_size("tile")]).astype(jnp.int32)

    onward = [(i, i + 1) for i in range(lax.axis_size("req") * lax.axis_size("span") - 1)]
    count = lax.axis_size("tile")
    down = [(i, i + 1) for i in range(count - 1)]
    up = [(i + 1, i) for i in range(count - 1)]
    swap = [(i, i ^ 1) for i in range(count)]
    core = tile % 2
    first_core = core == 0

    def after(value, *others):
        return lax.optimization_barrier((value, *others))[0]

    def fold(value, axis, partner):
        return value + lax.ppermute(value, axis, partner)

    ring = lambda step: [(i, i ^ 1 if step == 0 else 3 - i) for i in range(4)]
    rung = lambda step: [
        (i, 2 * (i // 2 ^ 1 if step == 0 else 3 - i // 2) + i % 2) for i in range(count)
    ]

    late = rows - EARLY
    near_send = lax.dynamic_slice_in_dim(latents[1], late * (1 - core), EARLY, axis=0)
    near_rows = lax.ppermute(near_send, spread, onward)
    total = local_stats(frame_counts, place, latents, per_group)
    total = fold(total, "tile", swap)
    total = fold(total, "tile", rung(0))
    total = fold(total, "tile", rung(1))
    top = lax.ppermute(after(latents[:, -1], total), "tile", down)
    total = fold(total, "req", ring(0))
    bottom = lax.ppermute(after(latents[:, 0], total), "tile", up)
    total = fold(total, "req", ring(1))
    total = fold(total, "span", ring(0))
    pair_send = jnp.where(
        first_core,
        jnp.concatenate([top[1:], latents[1, :late], top[:1], latents[0, rows - 1 :]]),
        jnp.concatenate([latents[1, EARLY:], bottom[1:], bottom[:1], latents[0, :1]]),
    )
    far_send = lax.dynamic_slice_in_dim(latents[0], core, rows - 1, axis=0)
    near_rows, total = lax.optimization_barrier((near_rows, total))
    inner_send = jnp.where(first_core, near_rows[EARLY - 1], near_rows[0])[None]
    inner_1 = lax.ppermute(inner_send, "tile", swap)
    other = lax.ppermute(total, "span", ring(1))
    pair_rows = lax.ppermute(pair_send, spread, onward)
    far_rows = lax.ppermute(far_send, spread, onward)
    total = total + other

    cells_per_frame = rows * count * cols * per_group
    weight = conv_weight.reshape(3, 3, 3 * channels, channels)
    gain, shift, bias = (v.reshape(1, channels) for v in (norm_gain, norm_shift, conv_bias))
    run = functools.partial(conv_stage, per_group=per_group, cells_per_frame=cells_per_frame)
    near = (top, bottom)
    middle = (top, bottom, near_rows, pair_rows, inner_1)
    affine, acc = run("a", frame_counts, place, latents, near, weight, (total, gain, shift))
    pair_rows, acc = lax.optimization_barrier((pair_rows, acc))
    inner_0 = lax.ppermute(pair_rows[late + 2 :], "tile", swap)
    acc, decoded = run("b", frame_counts, place, latents, middle[:3] + (pair_rows, inner_1), weight, (affine, bias), acc)
    far = (top, bottom, near_rows, pair_rows, inner_1, far_rows, inner_0)
    return run("c", frame_counts, place, latents, far, weight, (affine, bias), acc, decoded)


def solution(mesh):
    placed = (P(("req", "span"), "tile", None, None), P(), P(), P(), P(), P())
    return jax.shard_map(
        shards,
        mesh=mesh,
        in_specs=placed,
        out_specs=P(("req", "span"), "tile", None, None),
        check_vma=False,
    )
```
